256 devices in a mesh: sub: 8 (over x, core), tm: 32 (over z, y).
Axes of the slice: x: 4, y: 4, z: 8, core: 2. Of those that a mesh axis runs over, the one named last changes fastest.
Arguments:
- spectra: bfloat16 [2048, 131072], P('sub', 'tm'), may hold values from -2000 to 2000
- chan_mask: int32 [2048], P('sub'), may hold values from 0 to 1
- delay_step: int32 [2048], replicated, may hold values from 2 to 18, as said below
Outputs:
- peaks: float32 [512, 8, 512], P('sub', None, 'tm')
The draws below stay inside these ranges and needn't reach their ends.
Inputs may be any that keep to these rules, and one draw needn't show every extreme that they name: `delay_step`: non-decreasing in frequency order; the first entry is 2 and the last 18.
All inputs are finite; a program needn't handle non-finite values.
Results may differ from the reference program's by a relative error of at most 0.0003.
Values may be sent and summed in bfloat16 or wider, within the bound.
A program may use at most 64 MiB of HBM per device.

```python
import math
import jax
import jax.numpy as jnp
import numpy as np
from jax import lax

LOCAL = 8
CH_DEV = 256
CH = 2048
NDM = 512
TIME = 131072
WIDTHS = 8
BLOCK = 256
N_SUB = 8


def draw_spectra(key, part):
    key_chan, key_time, key_noise, key_offset = jax.random.split(key, 4)
    chan_scale = jnp.exp(jax.random.uniform(key_chan, (CH, 1), jnp.float32) * math.log(10.0))
    time_scale = jnp.exp(jax.random.uniform(key_time, (1, TIME), jnp.float32) * math.log(10.0))
    ramp = 1.0 + 2.0 * jnp.arange(TIME, dtype=jnp.float32)[None, :] / TIME
    noise = jnp.clip(jax.random.normal(key_noise, (CH, TIME), jnp.float32), -6.0, 6.0)
    offset = jax.random.uniform(key_offset, (CH, 1), jnp.float32, 0.5, 1.5)
    values = chan_scale * (time_scale * ramp * noise + offset * ramp)
    return values.astype(jnp.bfloat16)


def draw_chan_mask(key, part):
    threshold = 25 + 65 * jnp.arange(CH, dtype=jnp.int32) // CH
    return (jax.random.randint(key, (CH,), 0, 100) < threshold).astype(jnp.int32)


def draw_delay_step(key, part):
    rising = jnp.cumsum(jax.random.randint(key, (CH,), 1, 4)).astype(jnp.int32)
    total_rise = rising[CH - 1] - rising[0]
    return (2 + 16 * (rising - rising[0]) // total_rise).astype(jnp.int32)


def setup_inputs(seed: int = 0) -> dict:
    key_of = jax.random.split(jax.random.key(seed), 4)
    return {
        "spectra": draw_spectra(jax.random.fold_in(key_of[3], 71), 0),
        "chan_mask": draw_chan_mask(jax.random.fold_in(key_of[3], 71), 0),
        "delay_step": draw_delay_step(jax.random.fold_in(key_of[3], 71), 0),
    }


def reverse_index(number, bit_count):
    result = 0
    for bit_place in range(bit_count):
        result = result | (number >> bit_place & 1) << bit_count - 1 - bit_place
    return result

def split_shifts(prefix, starts, half_span, trial_ids):
    early_span = prefix[starts + half_span] - prefix[starts]
    later_span = prefix[starts + 2 * half_span] - prefix[starts + half_span]
    return trial_ids[None, :] * early_span[:, None] // (early_span + later_span)[:, None]

def slide_rows(row_block, amounts, length):

    def single(one_row, amount):
        return lax.dynamic_slice_in_dim(one_row, amount, length)
    return jax.vmap(jax.vmap(single, (None, 0)), (0, 0))(row_block, amounts)

def merge_pairs(planes, shifts):
    band_total, row_depth, columns = planes.shape
    paired = planes.reshape(band_total // 2, 2, row_depth, columns)
    lower_rows = paired[:, 0].reshape(-1, columns)
    upper_rows = jnp.pad(paired[:, 1].reshape(-1, columns), ((0, 0), (0, row_depth)))
    moved = slide_rows(upper_rows, shifts.reshape(-1, 2), columns)
    return (lower_rows[:, None, :] + moved).reshape(band_total // 2, 2 * row_depth, columns)

def reference(spectra, chan_mask, delay_step):
    cross_levels = N_SUB.bit_length() - 1
    block_order = np.array([reverse_index(block_pos, cross_levels) for block_pos in range(N_SUB)])
    ordered = spectra.reshape(N_SUB, CH_DEV, TIME)[block_order].reshape(CH, TIME)
    ordered_mask = chan_mask.reshape(N_SUB, CH_DEV)[block_order].reshape(CH)
    as_float = ordered.astype(jnp.float32)
    centre = lax.optimization_barrier(jnp.mean(as_float, axis=1))
    spread = lax.rsqrt(lax.optimization_barrier(jnp.mean(as_float * as_float, axis=1)) - centre * centre + 1e-05)
    normed = (as_float - centre[:, None]) * spread[:, None] * ordered_mask.astype(jnp.float32)[:, None]
    planes = lax.optimization_barrier(jnp.sum(normed.reshape(CH // 4, 4, TIME), axis=1))[:, None, :]
    prefix = jnp.concatenate([jnp.zeros((1,), jnp.int32), jnp.cumsum(delay_step).astype(jnp.int32)])
    for merge_level in range(3, LOCAL + cross_levels + 1):
        band_count = CH >> merge_level
        starts = jnp.arange(band_count, dtype=jnp.int32) * 2 ** merge_level
        trial_ids = jnp.arange(2 ** (merge_level - 2), dtype=jnp.int32)
        shifts = split_shifts(prefix, starts, 2 ** (merge_level - 1), trial_ids)
        planes = merge_pairs(planes, shifts)
    final_rows = planes[0]
    mean_power = lax.optimization_barrier(jnp.mean(final_rows * final_rows, axis=1))
    scaled = final_rows / jnp.sqrt(mean_power + 1e-06)[:, None]
    widest = 2 ** (WIDTHS - 1)
    running = jnp.pad(scaled, ((0, 0), (widest - 1, 0)))
    maxima = []
    for section in range(WIDTHS):
        box_width = 2 ** section
        if section > 0:
            running = running[:, box_width // 2:] + running[:, :-(box_width // 2)]
        snr_rows = running[:, -TIME:] / math.sqrt(box_width)
        maxima.append(lax.optimization_barrier(jnp.max(snr_rows.reshape(NDM, TIME // BLOCK, BLOCK), axis=2)))
    return jnp.stack(maxima, axis=1)
```

```python
import functools
import math

import jax
import jax.numpy as jnp
from jax import lax
from jax.experimental import pallas as pl
from jax.experimental.pallas import tpu as pltpu
from jax.sharding import PartitionSpec as P

MESH = pl.DeviceIdType.MESH
F32 = jnp.float32
BF16 = jnp.bfloat16
I32 = jnp.int32

WIDTHS = 8
LANES = 128
LEFT = 1
RIGHT = 4
SPAN = 40


def reversed_bits(number, bit_count):
    result = 0
    for place in range(bit_count):
        result = result + ((number >> place) % 2) * 2 ** (bit_count - 1 - place)
    return result


def iota(shape, dim):
    return lax.broadcasted_iota(I32, shape, dim)


def remote(src, dst, send_sem, recv_sem, device_id):
    return pltpu.make_async_remote_copy(
        src_ref=src,
        dst_ref=dst,
        send_sem=send_sem,
        recv_sem=recv_sem,
        device_id=device_id,
        device_id_type=MESH,
    )


def delay_table(geo, position, sub_index, delay_ref):
    rows = geo.rows
    level_rows = []
    local = delay_ref[pl.ds(2 * position, 2), :].astype(F32)
    local = jnp.concatenate([local[0:1], local[1:2]], axis=1)
    local = jnp.broadcast_to(local, (8, geo.channels)).astype(BF16)
    channel = iota((rows, geo.channels), 1)
    row = iota((rows, geo.channels), 0)
    blocks = jnp.sum(delay_ref[...].astype(F32), axis=1, keepdims=True)
    block = iota((2 * geo.n_sub, rows), 0) // 2
    lane_row = iota((1, rows), 1)
    for level in range(4, geo.local_levels + geo.cross_levels + 1):
        if level <= geo.local_levels:
            depth = level - 2
            band = row >> depth
            spans = []
            for mask in ((channel >> (level - 1)) == 2 * band, (channel >> level) == band):
                spans.append(
                    lax.dot_general(
                        local, mask.astype(F32).astype(BF16), (((1,), (1,)), ((), ())), preferred_element_type=F32
                    )[0:1]
                )
            trial = lane_row & (2**depth - 1)
        else:
            depth = level - 2 - geo.cross_levels
            band = iota((2 * geo.n_sub, rows), 1) >> depth
            up = level - geo.local_levels
            spans = []
            for mask in ((block >> (up - 1)) == 2 * band, (block >> up) == band):
                spans.append(jnp.sum(jnp.where(mask, blocks, 0.0), axis=0, keepdims=True))
            trial = sub_index * 2**depth + (lane_row & (2**depth - 1))
        early = spans[0].astype(I32)
        whole = jnp.maximum(spans[1].astype(I32), 1)
        product = trial * early
        shift = (product.astype(F32) / whole.astype(F32)).astype(I32)
        rest = product - shift * whole
        shift = shift + jnp.where(rest >= whole, 1, 0) - jnp.where(rest < 0, 1, 0)
        level_rows.append(jnp.clip(shift, 0, 2 ** (level - 3) - 1))
    table = jnp.concatenate(level_rows, axis=0)
    return jnp.concatenate([table, table], axis=1)


def merge(geo, src, dst, table, level, fan, wide=False):
    lane = iota((SPAN, LANES), 1)
    step = geo.tiles

    def pair(p, carry):
        low = p + (p // fan) * fan
        base = low * step
        upper = base + fan * step
        lower_rows = src[pl.ds(base, SPAN), :]
        if not wide:
            here = src[pl.ds(upper, SPAN), :]
            after = src[pl.ds(upper + 1, SPAN), :]
        for i in range(2):
            shift = table[level - 4, 2 * p + i]
            if wide:
                start = upper + (shift >> 7)
                shift = shift & (LANES - 1)
                here = src[pl.ds(start, SPAN), :]
                after = src[pl.ds(start + 1, SPAN), :]
            mixed = jnp.where(lane >= shift, here, after)
            moved = pltpu.roll(mixed, (LANES - shift) & (LANES - 1), 1)
            dst[pl.ds((2 * p + i) * step, SPAN), :] = lower_rows + moved
        return carry

    lax.fori_loop(0, geo.rows // 2, pair, 0, unroll=2)


def first_merge(geo, src, dst, table):
    lane = iota((SPAN, LANES), 1)
    step = geo.tiles

    def band(s, carry):
        base = 2 * s * step
        lower_rows = src[pl.ds(base, SPAN), :]
        here = src[pl.ds(base + step, SPAN), :]
        after = src[pl.ds(base + step + 1, SPAN), :]
        for i in range(4):
            shift = table[0, 4 * s + i]
            mixed = jnp.where(lane >= shift, here, after)
            moved = pltpu.roll(mixed, (LANES - shift) & (LANES - 1), 1)
            dst[pl.ds((4 * s + i) * step, SPAN), :] = lower_rows + moved
        return carry

    lax.fori_loop(0, geo.rows // 4, band, 0)


class Ring:
    def __init__(self, slots, me, count, device, send, recv):
        self.slots, self.me, self.count, self.device = slots, me, count, device
        self.send, self.recv = send, recv

    def copy(self, k, slot):
        peer = lax.rem(self.me + k, self.count)
        return remote(
            self.slots.at[self.me], self.slots.at[slot], self.send.at[k], self.recv.at[slot], self.device(peer)
        )

    def start(self, value):
        self.slots[pl.ds(self.me, 1)] = value[None]
        for k in range(1, self.count):
            self.copy(k, self.me).start()

    def total(self):
        for k in range(1, self.count):
            source = lax.rem(self.me + k, self.count)
            self.copy(k, source).wait_recv()
        for k in range(1, self.count):
            self.copy(k, self.me).wait_send()
        return jnp.sum(self.slots[...], axis=0)


def kernel(
    geo,
    spectra_ref,
    mask_ref,
    delay_ref,
    out_ref,
    x,
    gram,
    stat_y,
    stat_z,
    power_y,
    power_z,
    table_v,
    table,
    thin,
    buf_b,
    buf_c,
    buf_d,
    got,
    best,
    load_sem,
    table_sem,
    halo_send,
    halo_recv,
    ring_send,
    ring_recv,
    swap_send,
    swap_recv,
    own_sem,
):
    tiles, own, rows = geo.tiles, geo.own, geo.rows
    sub_index = lax.axis_index("sub")
    tm_index = lax.axis_index("tm")
    z_index, y_index = tm_index // geo.ny, lax.rem(tm_index, geo.ny)
    position = reversed_bits(sub_index, geo.cross_levels)
    not_first = tm_index > 0
    not_last = tm_index < geo.ny * geo.nz - 1

    def along_y(peer):
        return {"tm": z_index * geo.ny + peer}

    def along_z(peer):
        return {"tm": peer * geo.ny + y_index}

    own_first = LEFT * LANES
    right_first = (LEFT + own) * LANES
    chunk = geo.samples // 4
    loads = []
    for i in range(4):
        loads.append(
            pltpu.make_async_copy(
                spectra_ref.at[:, pl.ds(i * chunk, chunk)],
                x.at[:, pl.ds(own_first + i * chunk, chunk)],
                load_sem.at[i],
            )
        )
        loads[-1].start()

    barrier = pltpu.get_barrier_semaphore()
    for k in range(1, geo.ny):
        pl.semaphore_signal(barrier, inc=1, device_id=along_y(lax.rem(y_index + k, geo.ny)), device_id_type=MESH)
    for k in range(1, geo.nz):
        pl.semaphore_signal(barrier, inc=1, device_id=along_z(lax.rem(z_index + k, geo.nz)), device_id_type=MESH)
    for k in range(1, geo.n_sub):
        pl.semaphore_signal(
            barrier, inc=1, device_id={"sub": lax.rem(sub_index + k, geo.n_sub)}, device_id_type=MESH
        )

    n_tm = geo.ny * geo.nz
    for k in (1, n_tm - 1):
        pl.semaphore_signal(barrier, inc=1, device_id={"tm": lax.rem(tm_index + k, n_tm)}, device_id_type=MESH)
    pl.semaphore_wait(barrier, geo.ny + geo.nz + geo.n_sub - 1)

    def to_prev():
        return remote(
            spectra_ref.at[:, pl.ds(0, RIGHT * LANES)],
            x.at[:, pl.ds(right_first, RIGHT * LANES)],
            halo_send.at[0],
            halo_recv.at[0],
            {"tm": tm_index - 1},
        )

    def to_next():
        return remote(
            spectra_ref.at[:, pl.ds(geo.samples - LEFT * LANES, LEFT * LANES)],
            x.at[:, pl.ds(0, LEFT * LANES)],
            halo_send.at[1],
            halo_recv.at[1],
            {"tm": tm_index + 1},
        )

    @pl.when(not_first)
    def _():
        to_prev().start()

    @pl.when(not_last)
    def _():
        to_next().start()

    sums = jnp.zeros((8, geo.channels), F32)
    for i in range(4):
        loads[i].wait()
        part = x[:, pl.ds(own_first + i * chunk, chunk)]
        nt = (((1,), (1,)), ((), ()))
        square = lax.dot_general(part, part, nt, preferred_element_type=F32)
        if i == 0:
            gram[...] = square
        else:
            gram[...] += square
        sums = sums + lax.dot_general(jnp.ones((8, chunk), BF16), part, nt, preferred_element_type=F32)
    diagonal = iota((geo.channels, geo.channels), 0) == iota((geo.channels, geo.channels), 1)
    squares = jnp.sum(jnp.where(diagonal, gram[...], 0.0), axis=0, keepdims=True)
    half = geo.channels // 2
    stats = jnp.concatenate(
        [sums[0:1, :half], sums[0:1, half:], squares[:, :half], squares[:, half:], jnp.zeros((4, half), F32)], axis=0
    )
    over_y = Ring(stat_y, y_index, geo.ny, along_y, ring_send.at[0], ring_recv.at[0])
    over_z = Ring(stat_z, z_index, geo.nz, along_z, ring_send.at[1], ring_recv.at[1])
    over_y.start(stats)

    table_v[...] = delay_table(geo, position, sub_index, delay_ref)
    table_copy = pltpu.make_async_copy(table_v, table, table_sem)
    table_copy.start()

    over_z.start(over_y.total())

    @pl.when(jnp.logical_not(not_first))
    def _():
        x[:, pl.ds(0, LEFT * LANES)] = jnp.zeros((geo.channels, LEFT * LANES), BF16)

    @pl.when(jnp.logical_not(not_last))
    def _():
        x[:, pl.ds(right_first, RIGHT * LANES)] = jnp.zeros((geo.channels, RIGHT * LANES), BF16)

    totals = over_z.total()
    table_copy.wait()
    total_time = geo.samples * geo.ny * geo.nz
    centre = jnp.concatenate([totals[0:1], totals[1:2]], axis=1) / total_time
    power = jnp.concatenate([totals[2:3], totals[3:4]], axis=1) / total_time
    spread = lax.rsqrt(power - centre * centre + 1e-05)
    weight = spread * mask_ref[...].astype(F32)
    bands = geo.channels // 8
    member = iota((bands, geo.channels), 1) // 8 == iota((bands, geo.channels), 0)
    gain = jnp.where(member, weight, 0.0)
    gain_1 = gain.astype(BF16)
    rest = gain - gain_1.astype(F32)
    gain_2 = rest.astype(BF16)
    gain_3 = (rest - gain_2.astype(F32)).astype(BF16)
    gains = jnp.concatenate([gain_1, gain_2, gain_3], axis=0)
    offset = -jnp.sum(gain * centre, axis=1, keepdims=True)

    def normalise(first, count, shift):
        sample = jnp.dot(gains, x[:, pl.ds(first * LANES, count * LANES)], preferred_element_type=F32)
        value = sample[:bands] + sample[bands : 2 * bands] + sample[2 * bands :] + shift
        for g in range(bands // 8):
            for j in range(count):
                thin[pl.ds(8 * g * tiles + first + j, 8, stride=tiles), :] = value[
                    8 * g : 8 * g + 8, j * LANES : (j + 1) * LANES
                ]

    for i in range(own // 4):
        normalise(LEFT + 4 * i, 4, offset)

    @pl.when(not_first)
    def _():
        to_prev().wait_send()
        to_next().wait_recv()

    @pl.when(not_last)
    def _():
        to_next().wait_send()
        to_prev().wait_recv()

    normalise(0, LEFT, jnp.where(not_first, offset, 0.0))
    normalise(LEFT + own, RIGHT, jnp.where(not_last, offset, 0.0))

    first_merge(geo, thin, buf_b, table)
    buffers = [buf_b, buf_c]
    for level in range(5, geo.local_levels + 1):
        src, dst = buffers
        merge(geo, src, dst, table, level, 2 ** (level - 3))
        buffers = [dst, src]
    local_plane, spare = buffers

    share = rows // geo.n_sub * tiles

    def swap(k, slot):
        peer = lax.rem(sub_index + k, geo.n_sub)
        return remote(
            local_plane.at[pl.ds(peer * share, share), :],
            got.at[pl.ds(slot * share, share), :],
            swap_send.at[k],
            swap_recv.at[slot],
            {"sub": peer},
        )

    for k in range(1, geo.n_sub):
        swap(k, position).start()
    keep = pltpu.make_async_copy(
        local_plane.at[pl.ds(sub_index * share, share), :], got.at[pl.ds(position * share, share), :], own_sem
    )
    keep.start()
    for k in range(1, geo.n_sub):
        source = lax.rem(sub_index + k, geo.n_sub)
        swap(k, reversed_bits(source, geo.cross_levels)).wait_recv()
    for k in range(1, geo.n_sub):
        swap(k, position).wait_send()
    keep.wait()

    src, dst, other = got, spare, buf_d
    for up in range(1, geo.cross_levels + 1):
        level = geo.local_levels + up
        merge(geo, src, dst, table, level, rows // geo.n_sub * 2 ** (up - 1), wide=level >= 11)
        src, dst, other = dst, other, dst
    final = src

    lane = iota((8, LANES), 1)

    def group_tile(g, j):
        return final[pl.ds(8 * g * tiles + j, 8, stride=tiles), :]

    def group_power(g, packed):
        total = jnp.zeros((8, LANES), F32)
        for j in range(LEFT, LEFT + own):
            tile = group_tile(g, j)
            total = total + tile * tile
        return jnp.where(lane == g, jnp.sum(total, axis=1, keepdims=True), packed)

    packed = lax.fori_loop(0, rows // 8, group_power, jnp.zeros((8, LANES), F32))
    over_y = Ring(power_y, y_index, geo.ny, along_y, ring_send.at[2], ring_recv.at[2])
    over_z = Ring(power_z, z_index, geo.nz, along_z, ring_send.at[3], ring_recv.at[3])
    over_y.start(packed)

    def group_best(g, carry):
        box = [jnp.where(not_first, group_tile(g, 0), 0.0)]
        box += [group_tile(g, j) for j in range(1, LEFT + own)]
        for section in range(WIDTHS):
            if section > 0:
                lag = 2 ** (section - 1)
                near = lane < LANES - lag
                for j in range(LEFT + own - 1, -1, -1):
                    mixed = jnp.where(near, box[j], box[max(j - 1, 0)])
                    box[j] = box[j] + pltpu.roll(mixed, lag, 1)
            found = [jnp.maximum(box[LEFT + 2 * b], box[LEFT + 2 * b + 1]) for b in range(own // 2)]
            step = 1
            while len(found) > 1:
                even = (lane & step) == 0
                found = [
                    jnp.maximum(jnp.where(even, a, b), pltpu.roll(jnp.where(even, b, a), step, 1))
                    for a, b in zip(found[::2], found[1::2])
                ]
                step *= 2
            largest = found[0]
            while step < LANES:
                largest = jnp.maximum(largest, pltpu.roll(largest, step, 1))
                step *= 2
            best[pl.ds(pl.multiple_of(section * rows + 8 * g, 8), 8), :] = largest
        return carry

    groups = rows // 8
    lax.fori_loop(0, groups // 2, group_best, 0)
    over_z.start(over_y.total())
    lax.fori_loop(groups // 2, groups, group_best, 0)
    mean_power = over_z.total() / total_time
    inverse = 1.0 / jnp.sqrt(mean_power + 1e-06)
    for g in range(groups):
        scale = jnp.sum(jnp.where(lane == g, inverse, 0.0), axis=1, keepdims=True)
        for section in range(WIDTHS):
            value = best[section * rows + 8 * g : section * rows + 8 * g + 8, :]
            buf_d[pl.ds(8 * WIDTHS * g + section, 8, stride=WIDTHS), :] = value * (
                scale * (1.0 / math.sqrt(2**section))
            )
    out_ref[...] = buf_d[0 : rows * WIDTHS, 0 : own // 2]


class Geometry:
    pass


def local(mesh, spectra, chan_mask, delay_step):
    geo = Geometry()
    geo.n_sub = mesh.shape["sub"]
    n_tm = mesh.shape["tm"]
    geo.ny = 4 if n_tm % 4 == 0 else n_tm
    geo.nz = n_tm // geo.ny
    geo.channels, geo.samples = spectra.shape
    geo.cross_levels = geo.n_sub.bit_length() - 1
    geo.local_levels = geo.channels.bit_length() - 1
    geo.rows = geo.channels // 4
    geo.own = geo.samples // LANES
    geo.tiles = LEFT + geo.own + RIGHT
    tall = geo.rows * geo.tiles + 64
    dma = pltpu.SemaphoreType.DMA
    slots = max(geo.ny, geo.nz)
    best = pl.pallas_call(
        functools.partial(kernel, geo),
        out_shape=jax.ShapeDtypeStruct((geo.rows * WIDTHS, geo.own // 2), F32),
        in_specs=[
            pl.BlockSpec(memory_space=pl.ANY),
            pl.BlockSpec(memory_space=pltpu.VMEM),
            pl.BlockSpec(memory_space=pltpu.VMEM),
        ],
        out_specs=pl.BlockSpec(memory_space=pltpu.VMEM),
        scratch_shapes=[
            pltpu.VMEM((geo.channels, geo.tiles * LANES), BF16),
            pltpu.VMEM((geo.channels, geo.channels), F32),
            pltpu.VMEM((geo.ny, 8, LANES), F32),
            pltpu.VMEM((geo.nz, 8, LANES), F32),
            pltpu.VMEM((geo.ny, 8, LANES), F32),
            pltpu.VMEM((geo.nz, 8, LANES), F32),
            pltpu.VMEM((8, LANES), I32),
            pltpu.SMEM((8, LANES), I32),
            pltpu.VMEM((geo.rows // 2 * geo.tiles + 64, LANES), F32),
            pltpu.VMEM((tall, LANES), F32),
            pltpu.VMEM((tall, LANES), F32),
            pltpu.VMEM((tall, LANES), F32),
            pltpu.VMEM((tall, LANES), F32),
            pltpu.VMEM((geo.rows * WIDTHS, LANES), F32),
            dma((4,)),
            dma(()),
            dma((2,)),
            dma((2,)),
            dma((4, slots)),
            dma((4, slots)),
            dma((geo.n_sub,)),
            dma((geo.n_sub,)),
            dma(()),
        ],
        compiler_params=pltpu.CompilerParams(collective_id=0, has_side_effects=True, vmem_limit_bytes=48 * 2**20),
        name="dedisperse",
    )(spectra, chan_mask.reshape(1, geo.channels), delay_step.reshape(-1, LANES))
    return best.reshape(geo.rows, WIDTHS, geo.own // 2)


def solution(mesh):
    in_specs = (P("sub", "tm"), P("sub"), P())
    out_specs = P("sub", None, "tm")
    return jax.shard_map(
        functools.partial(local, mesh), mesh=mesh, in_specs=in_specs, out_specs=out_specs, check_vma=False
    )
```

```python
import functools
import math

import jax
import jax.numpy as jnp
from jax import lax
from jax.experimental import pallas as pl
from jax.experimental.pallas import tpu as pltpu
from jax.sharding import PartitionSpec as P

MESH = pl.DeviceIdType.MESH
F32 = jnp.float32
BF16 = jnp.bfloat16
I32 = jnp.int32

WIDTHS = 8
LANES = 128
LEFT = 1
RIGHT = 4
CODE = 32767.0
SPAN = 40


def reversed_bits(number, bit_count):
    result = 0
    for place in range(bit_count):
        result = result + ((number >> place) % 2) * 2 ** (bit_count - 1 - place)
    return result


def iota(shape, dim):
    return lax.broadcasted_iota(I32, shape, dim)


def remote(src, dst, send_sem, recv_sem, device_id):
    return pltpu.make_async_remote_copy(
        src_ref=src,
        dst_ref=dst,
        send_sem=send_sem,
        recv_sem=recv_sem,
        device_id=device_id,
        device_id_type=MESH,
    )


def delay_table(geo, position, sub_index, delay_ref):
    rows = geo.rows
    level_rows = []
    local = delay_ref[pl.ds(2 * position, 2), :].astype(F32)
    local = jnp.concatenate([local[0:1], local[1:2]], axis=1)
    local = jnp.broadcast_to(local, (8, geo.channels)).astype(BF16)
    channel = iota((rows, geo.channels), 1)
    row = iota((rows, geo.channels), 0)
    blocks = jnp.sum(delay_ref[...].astype(F32), axis=1, keepdims=True)
    block = iota((2 * geo.n_sub, rows), 0) // 2
    lane_row = iota((1, rows), 1)
    for level in range(4, geo.local_levels + geo.cross_levels + 1):
        if level <= geo.local_levels:
            depth = level - 2
            band = row >> depth
            spans = []
            for mask in ((channel >> (level - 1)) == 2 * band, (channel >> level) == band):
                spans.append(
                    lax.dot_general(
                        local, mask.astype(F32).astype(BF16), (((1,), (1,)), ((), ())), preferred_element_type=F32
                    )[0:1]
                )
            trial = lane_row & (2**depth - 1)
        else:
            depth = level - 2 - geo.cross_levels
            band = iota((2 * geo.n_sub, rows), 1) >> depth
            up = level - geo.local_levels
            spans = []
            for mask in ((block >> (up - 1)) == 2 * band, (block >> up) == band):
                spans.append(jnp.sum(jnp.where(mask, blocks, 0.0), axis=0, keepdims=True))
            trial = sub_index * 2**depth + (lane_row & (2**depth - 1))
        early = spans[0].astype(I32)
        whole = jnp.maximum(spans[1].astype(I32), 1)
        product = trial * early
        shift = (product.astype(F32) / whole.astype(F32)).astype(I32)
        rest = product - shift * whole
        shift = shift + jnp.where(rest >= whole, 1, 0) - jnp.where(rest < 0, 1, 0)
        level_rows.append(jnp.clip(shift, 0, 2 ** (level - 3) - 1))
    table = jnp.concatenate(level_rows, axis=0)
    return jnp.concatenate([table, table], axis=1)


def merge(geo, src, dst, table, level, fan, wide=False):
    lane = iota((SPAN, LANES), 1)
    step = geo.tiles

    def pair(p, carry):
        low = p + (p // fan) * fan
        base = low * step
        upper = base + fan * step
        lower_rows = src[pl.ds(base, SPAN), :]
        if not wide:
            here = src[pl.ds(upper, SPAN), :]
            after = src[pl.ds(upper + 1, SPAN), :]
        for i in range(2):
            shift = table[level - 4, 2 * p + i]
            if wide:
                start = upper + (shift >> 7)
                shift = shift & (LANES - 1)
                here = src[pl.ds(start, SPAN), :]
                after = src[pl.ds(start + 1, SPAN), :]
            mixed = jnp.where(lane >= shift, here, after)
            moved = pltpu.roll(mixed, (LANES - shift) & (LANES - 1), 1)
            dst[pl.ds((2 * p + i) * step, SPAN), :] = lower_rows + moved
        return carry

    lax.fori_loop(0, geo.rows // 2, pair, 0, unroll=16)


def first_merge(geo, src, dst, table):
    lane = iota((SPAN, LANES), 1)
    step = geo.tiles

    def band(s, carry):
        base = 2 * s * step
        lower_rows = src[pl.ds(base, SPAN), :]
        here = src[pl.ds(base + step, SPAN), :]
        after = src[pl.ds(base + step + 1, SPAN), :]
        for i in range(4):
            shift = table[0, 4 * s + i]
            mixed = jnp.where(lane >= shift, here, after)
            moved = pltpu.roll(mixed, (LANES - shift) & (LANES - 1), 1)
            dst[pl.ds((4 * s + i) * step, SPAN), :] = lower_rows + moved
        return carry

    lax.fori_loop(0, geo.rows // 4, band, 0, unroll=8)


class Ring:
    def __init__(self, slots, me, count, device, send, recv):
        self.slots, self.me, self.count, self.device = slots, me, count, device
        self.send, self.recv = send, recv

    def copy(self, k, slot):
        peer = lax.rem(self.me + k, self.count)
        return remote(
            self.slots.at[self.me], self.slots.at[slot], self.send.at[k], self.recv.at[slot], self.device(peer)
        )

    def start(self, value):
        self.slots[pl.ds(self.me, 1)] = value[None]
        for k in range(1, self.count):
            self.copy(k, self.me).start()

    def total(self):
        for k in range(1, self.count):
            source = lax.rem(self.me + k, self.count)
            self.copy(k, source).wait_recv()
        for k in range(1, self.count):
            self.copy(k, self.me).wait_send()
        return jnp.sum(self.slots[...], axis=0)


def along(values, index, axis):
    numbers = lax.GatherDimensionNumbers(
        offset_dims=(),
        collapsed_slice_dims=(axis,),
        start_index_map=(axis,),
        operand_batching_dims=(1 - axis,),
        start_indices_batching_dims=(1 - axis,),
    )
    return lax.gather(
        values, index[..., None], numbers, slice_sizes=(1, 1), mode=lax.GatherScatterMode.PROMISE_IN_BOUNDS
    )


def kernel(
    geo,
    spectra_ref,
    mask_hbm,
    delay_hbm,
    out_ref,
    x,
    gram,
    stat_y,
    stat_z,
    power_y,
    power_z,
    table_v,
    table,
    thin,
    plane,
    other,
    coded,
    coded_scale,
    got,
    got_scale,
    best,
    mask_ref,
    delay_ref,
    load_sem,
    small_sem,
    table_sem,
    halo_send,
    halo_recv,
    ring_send,
    ring_recv,
    swap_send,
    swap_recv,
    own_sem,
):
    tiles, own = geo.tiles, geo.own
    sub_index = lax.axis_index("sub")
    tm_index = lax.axis_index("tm")
    z_index, y_index = tm_index // geo.ny, lax.rem(tm_index, geo.ny)
    position = reversed_bits(sub_index, 3)
    n_tm = geo.ny * geo.nz
    not_first = tm_index > 0
    not_last = tm_index < n_tm - 1
    lane = iota((8, LANES), 1)

    def along_y(peer):
        return {"tm": z_index * geo.ny + peer}

    def along_z(peer):
        return {"tm": peer * geo.ny + y_index}

    barrier = pltpu.get_barrier_semaphore()
    for k in range(1, geo.ny):
        pl.semaphore_signal(barrier, inc=1, device_id=along_y(lax.rem(y_index + k, geo.ny)), device_id_type=MESH)
    for k in range(1, geo.nz):
        pl.semaphore_signal(barrier, inc=1, device_id=along_z(lax.rem(z_index + k, geo.nz)), device_id_type=MESH)
    for k in range(1, geo.n_sub):
        pl.semaphore_signal(
            barrier, inc=1, device_id={"sub": lax.rem(sub_index + k, geo.n_sub)}, device_id_type=MESH
        )
    for k in (1, n_tm - 1):
        pl.semaphore_signal(barrier, inc=1, device_id={"tm": lax.rem(tm_index + k, n_tm)}, device_id_type=MESH)

    own_first = LEFT * LANES
    right_first = (LEFT + own) * LANES
    chunk = geo.samples // 4
    loads = []
    for i in range(4):
        loads.append(
            pltpu.make_async_copy(
                spectra_ref.at[:, pl.ds(i * chunk, chunk)],
                x.at[:, pl.ds(own_first + i * chunk, chunk)],
                load_sem.at[i],
            )
        )
        loads[-1].start()
    small = [
        pltpu.make_async_copy(mask_hbm, mask_ref, small_sem.at[0]),
        pltpu.make_async_copy(delay_hbm, delay_ref, small_sem.at[1]),
    ]
    for copy in small:
        copy.start()

    sums = jnp.zeros((8, geo.channels), F32)
    nt = (((1,), (1,)), ((), ()))
    for i in range(4):
        loads[i].wait()
        part = x[:, pl.ds(own_first + i * chunk, chunk)]
        square = lax.dot_general(part, part, nt, preferred_element_type=F32)
        if i == 0:
            gram[...] = square
        else:
            gram[...] += square
        sums = sums + lax.dot_general(jnp.ones((8, chunk), BF16), part, nt, preferred_element_type=F32)
    diagonal = iota((geo.channels, geo.channels), 0) == iota((geo.channels, geo.channels), 1)
    squares = jnp.sum(jnp.where(diagonal, gram[...], 0.0), axis=0, keepdims=True)
    half = geo.channels // 2
    stats = jnp.concatenate(
        [sums[0:1, :half], sums[0:1, half:], squares[:, :half], squares[:, half:], jnp.zeros((4, half), F32)], axis=0
    )
    pl.semaphore_wait(barrier, geo.ny + geo.nz + geo.n_sub - 1)
    over_y = Ring(stat_y, y_index, geo.ny, along_y, ring_send.at[0], ring_recv.at[0])
    over_z = Ring(stat_z, z_index, geo.nz, along_z, ring_send.at[1], ring_recv.at[1])
    over_y.start(stats)

    def to_prev():
        return remote(
            spectra_ref.at[:, pl.ds(0, RIGHT * LANES)],
            x.at[:, pl.ds(right_first, RIGHT * LANES)],
            halo_send.at[0],
            halo_recv.at[0],
            {"tm": tm_index - 1},
        )

    def to_next():
        return remote(
            spectra_ref.at[:, pl.ds(geo.samples - LEFT * LANES, LEFT * LANES)],
            x.at[:, pl.ds(0, LEFT * LANES)],
            halo_send.at[1],
            halo_recv.at[1],
            {"tm": tm_index + 1},
        )

    @pl.when(not_first)
    def _():
        to_prev().start()

    @pl.when(not_last)
    def _():
        to_next().start()

    @pl.when(jnp.logical_not(not_first))
    def _():
        x[:, pl.ds(0, LEFT * LANES)] = jnp.zeros((geo.channels, LEFT * LANES), BF16)

    @pl.when(jnp.logical_not(not_last))
    def _():
        x[:, pl.ds(right_first, RIGHT * LANES)] = jnp.zeros((geo.channels, RIGHT * LANES), BF16)

    for copy in small:
        copy.wait()
    table_v[...] = delay_table(geo, position, sub_index, delay_ref)
    table_copy = pltpu.make_async_copy(table_v, table, table_sem)
    table_copy.start()
    over_z.start(over_y.total())

    totals = over_z.total()
    table_copy.wait()
    total_time = geo.samples * n_tm
    centre = jnp.concatenate([totals[0:1], totals[1:2]], axis=1) / total_time
    power = jnp.concatenate([totals[2:3], totals[3:4]], axis=1) / total_time
    spread = lax.rsqrt(power - centre * centre + 1e-05)
    weight = spread * mask_ref[...].astype(F32)
    bands = geo.channels // 8
    member = iota((bands, geo.channels), 1) // 8 == iota((bands, geo.channels), 0)
    gain = jnp.where(member, weight, 0.0)
    gain_1 = gain.astype(BF16)
    rest = gain - gain_1.astype(F32)
    gain_2 = rest.astype(BF16)
    gain_3 = (rest - gain_2.astype(F32)).astype(BF16)
    gains = jnp.concatenate([gain_1, gain_2, gain_3], axis=0)
    offset = -jnp.sum(gain * centre, axis=1, keepdims=True)

    def normalise(first, count, shift):
        sample = jnp.dot(gains, x[:, pl.ds(first * LANES, count * LANES)], preferred_element_type=F32)
        value = sample[:bands] + sample[bands : 2 * bands] + sample[2 * bands :] + shift
        for g in range(bands // 8):
            for j in range(count):
                thin[pl.ds(8 * g * tiles + first + j, 8, stride=tiles), :] = value[
                    8 * g : 8 * g + 8, j * LANES : (j + 1) * LANES
                ]

    for i in range(own // 4):
        normalise(LEFT + 4 * i, 4, offset)

    @pl.when(not_first)
    def _():
        to_prev().wait_send()
        to_next().wait_recv()

    @pl.when(not_last)
    def _():
        to_next().wait_send()
        to_prev().wait_recv()

    normalise(0, LEFT, jnp.where(not_first, offset, 0.0))
    normalise(LEFT + own, RIGHT, jnp.where(not_last, offset, 0.0))

    first_merge(geo, thin, plane, table)
    src, dst = plane, other
    for level in range(5, geo.local_levels + 1):
        merge(geo, src, dst, table, level, 2 ** (level - 3))
        src, dst = dst, src

    pairs = (tiles + 1) // 2

    def swap(k, peer, slot):
        return (
            remote(coded.at[peer], got.at[slot], swap_send.at[0, k], swap_recv.at[0, slot], {"sub": peer}),
            remote(
                coded_scale.at[peer], got_scale.at[slot], swap_send.at[1, k], swap_recv.at[1, slot], {"sub": peer}
            ),
        )

    def keep():
        return (
            pltpu.make_async_copy(coded.at[sub_index], got.at[position], own_sem.at[0]),
            pltpu.make_async_copy(coded_scale.at[sub_index], got_scale.at[position], own_sem.at[1]),
        )

    def piece(block, j):
        return pl.ds(pl.multiple_of(8 * (block * tiles + j), 8), 8)

    def column(j):
        return slice(j * LANES, (j + 1) * LANES)

    def send(k, carry):
        peer = lax.rem(sub_index + k, geo.n_sub)
        scales = jnp.zeros((8, LANES), F32)
        for j in range(pairs):
            one = src[piece(peer, j), :]
            two = src[piece(peer, min(j + pairs, tiles - 1)), :]
            largest = jnp.max(jnp.maximum(jnp.abs(one), jnp.abs(two)), axis=1, keepdims=True)
            largest = jnp.maximum(largest, 1e-30)
            factor = CODE / largest
            code = jnp.concatenate([one * factor, two * factor], axis=0)
            coded[pl.ds(peer, 1), :, column(j)] = jnp.round(code).astype(I32).astype(jnp.int16)[None]
            scales = jnp.where(lane == j, largest * (1.0 / CODE), scales)
        coded_scale[pl.ds(peer, 1)] = scales[None]

        @pl.when(k < geo.n_sub)
        def _():
            for copy in swap(k, peer, position):
                copy.start()

        @pl.when(k == geo.n_sub)
        def _():
            for copy in keep():
                copy.start()

        return carry

    lax.fori_loop(1, geo.n_sub + 1, send, 0)

    def decode(slot):
        scales = jnp.reshape(got_scale[pl.ds(slot, 1)], (8, LANES))
        for j in range(pairs):
            code = jnp.reshape(got[pl.ds(slot, 1), :, column(j)], (16, LANES)).astype(F32)
            scale = along(scales, jnp.full((8, LANES), j, I32), 1)
            dst[piece(slot, j), :] = code[0:8] * scale
            if j + pairs < tiles:
                dst[piece(slot, j + pairs), :] = code[8:16] * scale

    def receive(k, carry):
        source = lax.rem(sub_index - k + geo.n_sub, geo.n_sub)
        slot = reversed_bits(source, 3)
        for copy in swap(k, source, slot):
            copy.wait_recv()
        decode(slot)
        return carry

    for copy in keep():
        copy.wait()
    decode(position)
    lax.fori_loop(1, geo.n_sub, receive, 0)

    for level in range(9, 12):
        src, dst = dst, src
        merge(geo, src, dst, table, level, 2 ** (level - 6), wide=level == 11)
    final = dst

    def group_tile(g, j):
        return final[pl.ds(8 * g * tiles + j, 8, stride=tiles), :]

    def group_power(g, packed):
        total = jnp.zeros((8, LANES), F32)
        for j in range(LEFT, LEFT + own):
            tile = group_tile(g, j)
            total = total + tile * tile
        return jnp.where(lane == g, jnp.sum(total, axis=1, keepdims=True), packed)

    packed = lax.fori_loop(0, 8, group_power, jnp.zeros((8, LANES), F32), unroll=4)
    over_y = Ring(power_y, y_index, geo.ny, along_y, ring_send.at[2], ring_recv.at[2])
    over_z = Ring(power_z, z_index, geo.nz, along_z, ring_send.at[3], ring_recv.at[3])
    over_y.start(packed)

    def group_best(g, carry):
        box = [jnp.where(not_first, group_tile(g, 0), 0.0)]
        box += [group_tile(g, j) for j in range(1, LEFT + own)]
        kept = jnp.zeros((8, LANES), F32)
        for section in range(WIDTHS):
            if section > 0:
                lag = 2 ** (section - 1)
                near = lane < LANES - lag
                for j in range(LEFT + own - 1, -1, -1):
                    mixed = jnp.where(near, box[j], box[max(j - 1, 0)])
                    box[j] = box[j] + pltpu.roll(mixed, lag, 1)
            found = [jnp.maximum(box[LEFT + 2 * b], box[LEFT + 2 * b + 1]) for b in range(own // 2)]
            step = 1
            while len(found) > 1:
                even = (lane & step) == 0
                found = [
                    jnp.maximum(jnp.where(even, a, b), pltpu.roll(jnp.where(even, b, a), step, 1))
                    for a, b in zip(found[::2], found[1::2])
                ]
                step *= 2
            largest = found[0]
            while step < LANES:
                largest = jnp.maximum(largest, pltpu.roll(largest, step, 1))
                step *= 2
            kept = jnp.where((lane >> 4) == section, largest * (1.0 / math.sqrt(2**section)), kept)
        best[pl.ds(pl.multiple_of(8 * g, 8), 8), :] = kept
        return carry

    lax.fori_loop(0, 4, group_best, 0)
    over_z.start(over_y.total())
    lax.fori_loop(4, 8, group_best, 0)
    for k in range(1, geo.n_sub):
        for copy in swap(k, lax.rem(sub_index + k, geo.n_sub), position):
            copy.wait_send()
    mean_power = over_z.total() / total_time
    inverse = 1.0 / jnp.sqrt(mean_power + 1e-06)
    for g in range(8):
        scale = jnp.sum(jnp.where(lane == g, inverse, 0.0), axis=1, keepdims=True)
        best[8 * g : 8 * g + 8, :] = best[8 * g : 8 * g + 8, :] * scale
    out_ref[...] = best[...].T


class Geometry:
    pass


def local(mesh, spectra, chan_mask, delay_step):
    geo = Geometry()
    geo.n_sub = mesh.shape["sub"]
    n_tm = mesh.shape["tm"]
    geo.ny = 4
    geo.nz = n_tm // geo.ny
    geo.channels, geo.samples = spectra.shape
    geo.own = geo.samples // LANES
    geo.tiles = LEFT + geo.own + RIGHT
    assert (geo.n_sub, geo.channels, geo.own, geo.ny * geo.nz) == (8, 256, 32, n_tm)
    dma = pltpu.SemaphoreType.DMA
    slots = max(geo.ny, geo.nz)
    width = geo.tiles * LANES
    geo.rows, geo.local_levels, geo.cross_levels = 64, 8, 3
    pairs = (geo.tiles + 1) // 2
    anywhere = pl.BlockSpec(memory_space=pl.ANY)
    best = pl.pallas_call(
        functools.partial(kernel, geo),
        out_shape=jax.ShapeDtypeStruct((WIDTHS * geo.own // 2, 64), F32),
        in_specs=[anywhere, anywhere, anywhere],
        out_specs=pl.BlockSpec(memory_space=pltpu.VMEM),
        scratch_shapes=[
            pltpu.VMEM((geo.channels, width), BF16),
            pltpu.VMEM((geo.channels, geo.channels), F32),
            pltpu.VMEM((geo.ny, 8, LANES), F32),
            pltpu.VMEM((geo.nz, 8, LANES), F32),
            pltpu.VMEM((geo.ny, 8, LANES), F32),
            pltpu.VMEM((geo.nz, 8, LANES), F32),
            pltpu.VMEM((8, LANES), I32),
            pltpu.SMEM((8, LANES), I32),
            pltpu.VMEM((32 * geo.tiles + 64, LANES), F32),
            pltpu.VMEM((64 * geo.tiles + 64, LANES), F32),
            pltpu.VMEM((64 * geo.tiles + 64, LANES), F32),
            pltpu.VMEM((8, 16, pairs * LANES), jnp.int16),
            pltpu.VMEM((8, 8, LANES), F32),
            pltpu.VMEM((8, 16, pairs * LANES), jnp.int16),
            pltpu.VMEM((8, 8, LANES), F32),
            pltpu.VMEM((64, LANES), F32),
            pltpu.VMEM((1, geo.channels), I32),
            pltpu.VMEM((16, LANES), I32),
            dma((4,)),
            dma((2,)),
            dma(()),
            dma((2,)),
            dma((2,)),
            dma((4, slots)),
            dma((4, slots)),
            dma((2, geo.n_sub)),
            dma((2, geo.n_sub)),
            dma((2,)),
        ],
        compiler_params=pltpu.CompilerParams(collective_id=0, has_side_effects=True, vmem_limit_bytes=62 * 2**20),
        name="dedisperse",
    )(spectra, chan_mask.reshape(1, geo.channels), delay_step.reshape(16, LANES))
    return best.reshape(WIDTHS, geo.own // 2, 64).transpose(2, 0, 1)


def solution(mesh):
    in_specs = (P("sub", "tm"), P("sub"), P())
    out_specs = P("sub", None, "tm")
    return jax.shard_map(
        functools.partial(local, mesh), mesh=mesh, in_specs=in_specs, out_specs=out_specs, check_vma=False
    )
```

```python
import functools
import math

import jax
import jax.numpy as jnp
from jax import lax
from jax.experimental import pallas as pl
from jax.experimental.pallas import tpu as pltpu
from jax.sharding import PartitionSpec as P

MESH = pl.DeviceIdType.MESH
F32 = jnp.float32
BF16 = jnp.bfloat16
I32 = jnp.int32

WIDTHS = 8
LANES = 128
LEFT = 1
RIGHT = 4
SPAN = 40


def reversed_bits(number, bit_count):
    result = 0
    for place in range(bit_count):
        result = result + ((number >> place) % 2) * 2 ** (bit_count - 1 - place)
    return result


def iota(shape, dim):
    return lax.broadcasted_iota(I32, shape, dim)


def remote(src, dst, send_sem, recv_sem, device_id):
    return pltpu.make_async_remote_copy(
        src_ref=src,
        dst_ref=dst,
        send_sem=send_sem,
        recv_sem=recv_sem,
        device_id=device_id,
        device_id_type=MESH,
    )


def delay_table(geo, position, sub_index, delay_ref):
    rows = geo.rows
    level_rows = []
    local = delay_ref[pl.ds(2 * position, 2), :].astype(F32)
    local = jnp.concatenate([local[0:1], local[1:2]], axis=1)
    local = jnp.broadcast_to(local, (8, geo.channels)).astype(BF16)
    channel = iota((rows, geo.channels), 1)
    row = iota((rows, geo.channels), 0)
    blocks = jnp.sum(delay_ref[...].astype(F32), axis=1, keepdims=True)
    block = iota((2 * geo.n_sub, rows), 0) // 2
    lane_row = iota((1, rows), 1)
    for level in range(4, geo.local_levels + geo.cross_levels + 1):
        if level <= geo.local_levels:
            depth = level - 2
            band = row >> depth
            spans = []
            for mask in ((channel >> (level - 1)) == 2 * band, (channel >> level) == band):
                spans.append(
                    lax.dot_general(
                        local, mask.astype(F32).astype(BF16), (((1,), (1,)), ((), ())), preferred_element_type=F32
                    )[0:1]
                )
            trial = lane_row & (2**depth - 1)
        else:
            depth = level - 2 - geo.cross_levels
            band = iota((2 * geo.n_sub, rows), 1) >> depth
            up = level - geo.local_levels
            spans = []
            for mask in ((block >> (up - 1)) == 2 * band, (block >> up) == band):
                spans.append(jnp.sum(jnp.where(mask, blocks, 0.0), axis=0, keepdims=True))
            trial = sub_index * 2**depth + (lane_row & (2**depth - 1))
        early = spans[0].astype(I32)
        whole = jnp.maximum(spans[1].astype(I32), 1)
        product = trial * early
        shift = (product.astype(F32) / whole.astype(F32)).astype(I32)
        rest = product - shift * whole
        shift = shift + jnp.where(rest >= whole, 1, 0) - jnp.where(rest < 0, 1, 0)
        level_rows.append(jnp.clip(shift, 0, 2 ** (level - 3) - 1))
    table = jnp.concatenate(level_rows, axis=0)
    return jnp.concatenate([table, table], axis=1)


def move_rows(geo, src, steps, dst, lower, upper, shifts, outs, wide=False):
    lane = iota((SPAN, LANES), 1)
    from_step, to_step = steps
    lower_rows = src[pl.ds(lower * from_step, SPAN), :]
    start = upper * from_step
    if not wide:
        here = src[pl.ds(start, SPAN), :]
        after = src[pl.ds(start + 1, SPAN), :]
    for shift, out in zip(shifts, outs):
        if wide:
            tile = start + (shift >> 7)
            shift = shift & (LANES - 1)
            here = src[pl.ds(tile, SPAN), :]
            after = src[pl.ds(tile + 1, SPAN), :]
        mixed = jnp.where(lane >= shift, here, after)
        dst[pl.ds(out * to_step, SPAN), :] = lower_rows + pltpu.roll(mixed, (LANES - shift) & (LANES - 1), 1)


def merge(geo, src, dst, table, level, fan, half=None, to_step=SPAN):
    for s in range(32 // fan):
        for e in range(fan if half is None else fan // 2):
            first = e if half is None else half * (fan // 2) + e
            p = s * fan + first
            outs = [2 * p, 2 * p + 1]
            shifts = [table[level - 4, out] for out in outs]
            low = s * 2 * fan + first
            move_rows(geo, src, (SPAN, to_step), dst, low, low + fan, shifts, outs, wide=level == 11)


def first_merge(geo, src, dst, table):
    for s in range(16):
        outs = [4 * s + i for i in range(4)]
        shifts = [table[0, out] for out in outs]
        move_rows(geo, src, (geo.tiles, SPAN), dst, 2 * s, 2 * s + 1, shifts, outs)


class Ring:
    def __init__(self, slots, me, count, device, send, recv):
        self.slots, self.me, self.count, self.device = slots, me, count, device
        self.send, self.recv = send, recv

    def copy(self, k, slot):
        peer = lax.rem(self.me + k, self.count)
        return remote(
            self.slots.at[self.me], self.slots.at[slot], self.send.at[k], self.recv.at[slot], self.device(peer)
        )

    def start(self, value):
        self.slots[pl.ds(self.me, 1)] = value[None]
        for k in range(1, self.count):
            self.copy(k, self.me).start()

    def total(self):
        for k in range(1, self.count):
            source = lax.rem(self.me + k, self.count)
            self.copy(k, source).wait_recv()
        for k in range(1, self.count):
            self.copy(k, self.me).wait_send()
        return jnp.sum(self.slots[...], axis=0)


def along(values, index, axis):
    numbers = lax.GatherDimensionNumbers(
        offset_dims=(),
        collapsed_slice_dims=(axis,),
        start_index_map=(axis,),
        operand_batching_dims=(1 - axis,),
        start_indices_batching_dims=(1 - axis,),
    )
    return lax.gather(
        values, index[..., None], numbers, slice_sizes=(1, 1), mode=lax.GatherScatterMode.PROMISE_IN_BOUNDS
    )


def kernel(
    geo,
    spectra_ref,
    mask_hbm,
    delay_hbm,
    out_ref,
    x,
    gram,
    stat_y,
    stat_z,
    power_y,
    power_z,
    table_v,
    table,
    thin,
    plane,
    left,
    right,
    final,
    coded,
    got,
    best,
    mask_ref,
    delay_ref,
    load_sem,
    small_sem,
    table_sem,
    halo_send,
    halo_recv,
    ring_send,
    ring_recv,
    swap_send,
    swap_recv,
    own_sem,
):
    tiles, own = geo.tiles, geo.own
    sub_index = lax.axis_index("sub")
    tm_index = lax.axis_index("tm")
    z_index, y_index = tm_index // geo.ny, lax.rem(tm_index, geo.ny)
    position = reversed_bits(sub_index, 3)
    n_tm = geo.ny * geo.nz
    not_first = tm_index > 0
    not_last = tm_index < n_tm - 1
    lane = iota((8, LANES), 1)
    place = iota((8, LANES), 0)

    def along_y(peer):
        return {"tm": z_index * geo.ny + peer}

    def along_z(peer):
        return {"tm": peer * geo.ny + y_index}

    barrier = pltpu.get_barrier_semaphore()
    for k in range(1, geo.ny):
        pl.semaphore_signal(barrier, inc=1, device_id=along_y(lax.rem(y_index + k, geo.ny)), device_id_type=MESH)
    for k in range(1, geo.nz):
        pl.semaphore_signal(barrier, inc=1, device_id=along_z(lax.rem(z_index + k, geo.nz)), device_id_type=MESH)
    for k in range(1, geo.n_sub):
        pl.semaphore_signal(
            barrier, inc=1, device_id={"sub": lax.rem(sub_index + k, geo.n_sub)}, device_id_type=MESH
        )
    for k in (1, n_tm - 1):
        pl.semaphore_signal(barrier, inc=1, device_id={"tm": lax.rem(tm_index + k, n_tm)}, device_id_type=MESH)

    own_first = LEFT * LANES
    right_first = (LEFT + own) * LANES
    chunk = geo.samples // 4
    loads = []
    for i in range(4):
        loads.append(
            pltpu.make_async_copy(
                spectra_ref.at[:, pl.ds(i * chunk, chunk)],
                x.at[:, pl.ds(own_first + i * chunk, chunk)],
                load_sem.at[i],
            )
        )
        loads[-1].start()
    small = [
        pltpu.make_async_copy(mask_hbm, mask_ref, small_sem.at[0]),
        pltpu.make_async_copy(delay_hbm, delay_ref, small_sem.at[1]),
    ]
    for copy in small:
        copy.start()

    sums = jnp.zeros((8, geo.channels), F32)
    nt = (((1,), (1,)), ((), ()))
    for i in range(4):
        loads[i].wait()
        part = x[:, pl.ds(own_first + i * chunk, chunk)]
        square = lax.dot_general(part, part, nt, preferred_element_type=F32)
        if i == 0:
            gram[...] = square
        else:
            gram[...] += square
        sums = sums + lax.dot_general(jnp.ones((8, chunk), BF16), part, nt, preferred_element_type=F32)
    diagonal = iota((geo.channels, geo.channels), 0) == iota((geo.channels, geo.channels), 1)
    squares = jnp.sum(jnp.where(diagonal, gram[...], 0.0), axis=0, keepdims=True)
    half = geo.channels // 2
    stats = jnp.concatenate(
        [sums[0:1, :half], sums[0:1, half:], squares[:, :half], squares[:, half:]], axis=0
    )
    pl.semaphore_wait(barrier, geo.ny + geo.nz + geo.n_sub - 1)
    over_y = Ring(stat_y, y_index, geo.ny, along_y, ring_send.at[0], ring_recv.at[0])
    over_z = Ring(stat_z, z_index, geo.nz, along_z, ring_send.at[1], ring_recv.at[1])
    over_y.start(stats)

    def to_prev():
        return remote(
            spectra_ref.at[:, pl.ds(0, RIGHT * LANES)],
            x.at[:, pl.ds(right_first, RIGHT * LANES)],
            halo_send.at[0],
            halo_recv.at[0],
            {"tm": tm_index - 1},
        )

    def to_next():
        return remote(
            spectra_ref.at[:, pl.ds(geo.samples - LEFT * LANES, LEFT * LANES)],
            x.at[:, pl.ds(0, LEFT * LANES)],
            halo_send.at[1],
            halo_recv.at[1],
            {"tm": tm_index + 1},
        )

    @pl.when(not_first)
    def _():
        to_prev().start()

    @pl.when(not_last)
    def _():
        to_next().start()

    @pl.when(jnp.logical_not(not_first))
    def _():
        x[:, pl.ds(0, LEFT * LANES)] = jnp.zeros((geo.channels, LEFT * LANES), BF16)

    @pl.when(jnp.logical_not(not_last))
    def _():
        x[:, pl.ds(right_first, RIGHT * LANES)] = jnp.zeros((geo.channels, RIGHT * LANES), BF16)

    for copy in small:
        copy.wait()
    table_v[...] = delay_table(geo, position, sub_index, delay_ref)
    table_copy = pltpu.make_async_copy(table_v, table, table_sem)
    table_copy.start()
    over_z.start(over_y.total())

    totals = over_z.total()
    table_copy.wait()
    total_time = geo.samples * n_tm
    centre = jnp.concatenate([totals[0:1], totals[1:2]], axis=1) / total_time
    power = jnp.concatenate([totals[2:3], totals[3:4]], axis=1) / total_time
    spread = lax.rsqrt(power - centre * centre + 1e-05)
    weight = spread * mask_ref[...].astype(F32)
    bands = geo.channels // 8
    member = iota((bands, geo.channels), 1) // 8 == iota((bands, geo.channels), 0)
    gain = jnp.where(member, weight, 0.0)
    gain_1 = gain.astype(BF16)
    rest = gain - gain_1.astype(F32)
    gain_2 = rest.astype(BF16)
    gain_3 = (rest - gain_2.astype(F32)).astype(BF16)
    gains = jnp.concatenate([gain_1, gain_2, gain_3], axis=0)
    offset = -jnp.sum(gain * centre, axis=1, keepdims=True)

    def normalise(first, count, shift):
        sample = jnp.dot(gains, x[:, pl.ds(first * LANES, count * LANES)], preferred_element_type=F32)
        value = sample[:bands] + sample[bands : 2 * bands] + sample[2 * bands :] + shift
        for g in range(bands // 8):
            for j in range(count):
                thin[pl.ds(8 * g * tiles + first + j, 8, stride=tiles), :] = value[
                    8 * g : 8 * g + 8, j * LANES : (j + 1) * LANES
                ]

    for i in range(own // 4):
        normalise(LEFT + 4 * i, 4, offset)

    @pl.when(not_first)
    def _():
        to_prev().wait_send()
        to_next().wait_recv()

    @pl.when(not_last)
    def _():
        to_next().wait_send()
        to_prev().wait_recv()

    normalise(0, LEFT, jnp.where(not_first, offset, 0.0))
    normalise(LEFT + own, RIGHT, jnp.where(not_last, offset, 0.0))

    first_merge(geo, thin, plane, table)
    pairs = SPAN // 2

    def swap(k, peer, slot):
        return remote(coded.at[peer], got.at[slot], swap_send.at[k], swap_recv.at[slot], {"sub": peer})

    keep = pltpu.make_async_copy(coded.at[sub_index], got.at[position], own_sem)

    def piece(block, j):
        return pl.ds(pl.multiple_of(8 * (block * SPAN + j), 8), 8)

    def column(j):
        return slice(j * LANES, (j + 1) * LANES)

    def encode(peer):
        powers = jnp.zeros((8, LANES), F32)
        for j in range(pairs):
            one = right[piece(peer, j), :]
            two = right[piece(peer, j + pairs), :]
            largest = jnp.max(jnp.maximum(jnp.abs(one), jnp.abs(two)), axis=1, keepdims=True)
            power = jnp.ceil(jnp.log2(jnp.maximum(largest, 1e-30) * 1.001))
            factor = jnp.exp2(15.0 - power)
            code = jnp.concatenate([one * factor, two * factor], axis=0)
            coded[pl.ds(peer, 1), :, column(j)] = jnp.round(code).astype(I32).astype(jnp.int16)[None]
            powers = jnp.where(lane == j, power, powers)
        powers = jnp.concatenate([powers, powers], axis=0)
        coded[pl.ds(peer, 1), :, column(pairs)] = powers.astype(I32).astype(jnp.int16)[None]

    near = sub_index // 4
    far = 1 - near
    place_in_half = lax.rem(sub_index, 4)
    for half, first in ((far, 0), (near, 4)):
        merge(geo, plane, left, table, 5, 4, half)
        merge(geo, left, right, table, 6, 8, half)
        merge(geo, right, left, table, 7, 16, half)
        merge(geo, left, right, table, 8, 32, half)

        def send(k, carry):
            peer = 4 * half + lax.rem(place_in_half + k, 4)
            encode(peer)
            if first == 0:
                swap(first + k, peer, position).start()
            else:

                @pl.when(k < 4)
                def _():
                    swap(first + k, peer, position).start()

                @pl.when(k == 4)
                def _():
                    keep.start()

            return carry

        if first == 0:
            lax.fori_loop(0, 4, send, 0)
        else:
            lax.fori_loop(1, 5, send, 0)

    def decode(slot):
        block = got[pl.ds(slot, 1), :, column(pairs)]
        scales = jnp.exp2(jnp.reshape(block, (16, LANES)).astype(F32)[0:8] - 15.0)
        for j in range(pairs):
            code = jnp.reshape(got[pl.ds(slot, 1), :, column(j)], (16, LANES)).astype(F32)
            scale = along(scales, jnp.full((8, LANES), j, I32), 1)
            plane[piece(slot, j), :] = code[0:8] * scale
            plane[piece(slot, j + pairs), :] = code[8:16] * scale

    keep.wait()
    decode(position)

    def receive(source):
        slot = reversed_bits(source, 3)
        swap(0, source, slot).wait_recv()
        decode(slot)

    def receive_far(k, carry):
        receive(4 * far + lax.rem(place_in_half + 4 - k, 4))
        return carry

    def receive_near(k, carry):
        receive(4 * near + lax.rem(place_in_half + 4 - k, 4))
        return carry

    lax.fori_loop(0, 4, receive_far, 0)
    lax.fori_loop(1, 4, receive_near, 0)

    merge(geo, plane, left, table, 9, 8)
    merge(geo, left, right, table, 10, 16)
    merge(geo, right, final, table, 11, 32, to_step=tiles)

    def group_tile(g, j):
        return final[pl.ds(8 * g * tiles + j, 8, stride=tiles), :]

    def group_power(g, packed):
        total = jnp.zeros((8, LANES), F32)
        for j in range(LEFT, LEFT + own):
            tile = group_tile(g, j)
            total = total + tile * tile
        return jnp.where(lane == 8 * g + place, jnp.sum(total, axis=1, keepdims=True), packed)

    packed = lax.fori_loop(0, 8, group_power, jnp.zeros((8, LANES), F32), unroll=8)
    over_y = Ring(power_y, y_index, geo.ny, along_y, ring_send.at[2], ring_recv.at[2])
    over_z = Ring(power_z, z_index, geo.nz, along_z, ring_send.at[3], ring_recv.at[3])
    over_y.start(jnp.sum(packed, axis=0, keepdims=True))

    def group_best(g, carry):
        box = [jnp.where(not_first, group_tile(g, 0), 0.0)]
        box += [group_tile(g, j) for j in range(1, LEFT + own)]
        kept = jnp.zeros((8, LANES), F32)
        for section in range(WIDTHS):
            if section > 0:
                lag = 2 ** (section - 1)
                near = lane < LANES - lag
                for j in range(LEFT + own - 1, -1, -1):
                    mixed = jnp.where(near, box[j], box[max(j - 1, 0)])
                    box[j] = box[j] + pltpu.roll(mixed, lag, 1)
            found = [jnp.maximum(box[LEFT + 2 * b], box[LEFT + 2 * b + 1]) for b in range(own // 2)]
            step = 1
            while len(found) > 1:
                even = (lane & step) == 0
                found = [
                    jnp.maximum(jnp.where(even, a, b), pltpu.roll(jnp.where(even, b, a), step, 1))
                    for a, b in zip(found[::2], found[1::2])
                ]
                step *= 2
            largest = found[0]
            while step < LANES:
                largest = jnp.maximum(largest, pltpu.roll(largest, step, 1))
                step *= 2
            kept = jnp.where((lane >> 4) == section, largest * (1.0 / math.sqrt(2**section)), kept)
        best[pl.ds(pl.multiple_of(8 * g, 8), 8), :] = kept
        return carry

    lax.fori_loop(0, 4, group_best, 0)
    over_z.start(over_y.total())
    lax.fori_loop(4, 8, group_best, 0)
    for k in (0, 1, 2, 3, 5, 6, 7):
        swap(k, 4 * (far if k < 4 else near) + lax.rem(place_in_half + k, 4), position).wait_send()
    mean_power = over_z.total() / total_time
    inverse = jnp.broadcast_to(1.0 / jnp.sqrt(mean_power + 1e-06), (8, LANES))
    for g in range(8):
        scale = jnp.sum(jnp.where(lane == 8 * g + place, inverse, 0.0), axis=1, keepdims=True)
        best[8 * g : 8 * g + 8, :] = best[8 * g : 8 * g + 8, :] * scale
    out_ref[...] = best[...].T


class Geometry:
    pass


def local(mesh, spectra, chan_mask, delay_step):
    geo = Geometry()
    geo.n_sub = mesh.shape["sub"]
    n_tm = mesh.shape["tm"]
    geo.ny = 4
    geo.nz = n_tm // geo.ny
    geo.channels, geo.samples = spectra.shape
    geo.own = geo.samples // LANES
    geo.tiles = LEFT + geo.own + RIGHT
    assert (geo.n_sub, geo.channels, geo.own, geo.ny * geo.nz) == (8, 256, 32, n_tm)
    dma = pltpu.SemaphoreType.DMA
    slots = max(geo.ny, geo.nz)
    width = geo.tiles * LANES
    geo.rows, geo.local_levels, geo.cross_levels = 64, 8, 3
    anywhere = pl.BlockSpec(memory_space=pl.ANY)
    best = pl.pallas_call(
        functools.partial(kernel, geo),
        out_shape=jax.ShapeDtypeStruct((WIDTHS * geo.own // 2, 64), F32),
        in_specs=[anywhere, anywhere, anywhere],
        out_specs=pl.BlockSpec(memory_space=pltpu.VMEM),
        scratch_shapes=[
            pltpu.VMEM((geo.channels, width), BF16),
            pltpu.VMEM((geo.channels, geo.channels), F32),
            pltpu.VMEM((geo.ny, 4, LANES), F32),
            pltpu.VMEM((geo.nz, 4, LANES), F32),
            pltpu.VMEM((geo.ny, 1, LANES), F32),
            pltpu.VMEM((geo.nz, 1, LANES), F32),
            pltpu.VMEM((8, LANES), I32),
            pltpu.SMEM((8, LANES), I32),
            pltpu.VMEM((32 * geo.tiles + 64, LANES), F32),
            pltpu.VMEM((64 * SPAN + 16, LANES), F32),
            pltpu.VMEM((64 * SPAN + 16, LANES), F32),
            pltpu.VMEM((64 * SPAN + 16, LANES), F32),
            pltpu.VMEM((64 * geo.tiles + 64, LANES), F32),
            pltpu.VMEM((8, 16, (SPAN // 2 + 1) * LANES), jnp.int16),
            pltpu.VMEM((8, 16, (SPAN // 2 + 1) * LANES), jnp.int16),
            pltpu.VMEM((64, LANES), F32),
            pltpu.VMEM((1, geo.channels), I32),
            pltpu.VMEM((16, LANES), I32),
            dma((4,)),
            dma((2,)),
            dma(()),
            dma((2,)),
            dma((2,)),
            dma((4, slots)),
            dma((4, slots)),
            dma((geo.n_sub,)),
            dma((geo.n_sub,)),
            dma(()),
        ],
        compiler_params=pltpu.CompilerParams(collective_id=0, has_side_effects=True, vmem_limit_bytes=62 * 2**20),
        name="dedisperse",
    )(spectra, chan_mask.reshape(1, geo.channels), delay_step.reshape(16, LANES))
    return best.reshape(WIDTHS, geo.own // 2, 64).transpose(2, 0, 1)


def solution(mesh):
    in_specs = (P("sub", "tm"), P("sub"), P())
    out_specs = P("sub", None, "tm")
    return jax.shard_map(
        functools.partial(local, mesh), mesh=mesh, in_specs=in_specs, out_specs=out_specs, check_vma=False
    )
```

```python
import functools
import math

import jax
import jax.numpy as jnp
from jax import lax
from jax.experimental import pallas as pl
from jax.experimental.pallas import tpu as pltpu
from jax.sharding import PartitionSpec as P

MESH = pl.DeviceIdType.MESH
F32 = jnp.float32
BF16 = jnp.bfloat16
I32 = jnp.int32

WIDTHS = 8
LANES = 128
LEFT = 1
RIGHT = 4
SPAN = 40


def reversed_bits(number, bit_count):
    result = 0
    for place in range(bit_count):
        result = result + ((number >> place) % 2) * 2 ** (bit_count - 1 - place)
    return result


def iota(shape, dim):
    return lax.broadcasted_iota(I32, shape, dim)


def remote(src, dst, send_sem, recv_sem, device_id):
    return pltpu.make_async_remote_copy(
        src_ref=src,
        dst_ref=dst,
        send_sem=send_sem,
        recv_sem=recv_sem,
        device_id=device_id,
        device_id_type=MESH,
    )


def delay_table(geo, position, sub_index, delay_ref):
    rows = geo.rows
    level_rows = []
    local = delay_ref[pl.ds(2 * position, 2), :].astype(F32)
    local = jnp.concatenate([local[0:1], local[1:2]], axis=1)
    local = jnp.broadcast_to(local, (8, geo.channels)).astype(BF16)
    channel = iota((rows, geo.channels), 1)
    row = iota((rows, geo.channels), 0)
    blocks = jnp.sum(delay_ref[...].astype(F32), axis=1, keepdims=True)
    block = iota((2 * geo.n_sub, rows), 0) // 2
    lane_row = iota((1, rows), 1)
    for level in range(4, geo.local_levels + geo.cross_levels + 1):
        if level <= geo.local_levels:
            depth = level - 2
            band = row >> depth
            spans = []
            for mask in ((channel >> (level - 1)) == 2 * band, (channel >> level) == band):
                spans.append(
                    lax.dot_general(
                        local, mask.astype(F32).astype(BF16), (((1,), (1,)), ((), ())), preferred_element_type=F32
                    )[0:1]
                )
            trial = lane_row & (2**depth - 1)
        else:
            depth = level - 2 - geo.cross_levels
            band = iota((2 * geo.n_sub, rows), 1) >> depth
            up = level - geo.local_levels
            spans = []
            for mask in ((block >> (up - 1)) == 2 * band, (block >> up) == band):
                spans.append(jnp.sum(jnp.where(mask, blocks, 0.0), axis=0, keepdims=True))
            trial = sub_index * 2**depth + (lane_row & (2**depth - 1))
        early = spans[0].astype(I32)
        whole = jnp.maximum(spans[1].astype(I32), 1)
        product = trial * early
        shift = (product.astype(F32) / whole.astype(F32)).astype(I32)
        rest = product - shift * whole
        shift = shift + jnp.where(rest >= whole, 1, 0) - jnp.where(rest < 0, 1, 0)
        level_rows.append(jnp.clip(shift, 0, 2 ** (level - 3) - 1))
    table = jnp.concatenate(level_rows, axis=0)
    return jnp.concatenate([table, table], axis=1)


def move_rows(geo, src, steps, dst, lower, upper, shifts, outs, wide=False):
    lane = iota((SPAN, LANES), 1)
    from_step, to_step = steps
    lower_rows = src[pl.ds(lower * from_step, SPAN), :]
    start = upper * from_step
    if not wide:
        here = src[pl.ds(start, SPAN), :]
        after = src[pl.ds(start + 1, SPAN), :]
    for shift, out in zip(shifts, outs):
        if wide:
            tile = start + (shift >> 7)
            shift = shift & (LANES - 1)
            here = src[pl.ds(tile, SPAN), :]
            after = src[pl.ds(tile + 1, SPAN), :]
        mixed = jnp.where(lane >= shift, here, after)
        dst[pl.ds(out * to_step, SPAN), :] = lower_rows + pltpu.roll(mixed, (LANES - shift) & (LANES - 1), 1)


def merge(geo, src, dst, table, level, fan, half=None, to_step=SPAN):
    for s in range(32 // fan):
        for e in range(fan if half is None else fan // 2):
            first = e if half is None else half * (fan // 2) + e
            p = s * fan + first
            outs = [2 * p, 2 * p + 1]
            shifts = [table[level - 4, out] for out in outs]
            low = s * 2 * fan + first
            move_rows(geo, src, (SPAN, to_step), dst, low, low + fan, shifts, outs, wide=level == 11)


def first_merge(geo, src, dst, table):
    for s in range(16):
        outs = [4 * s + i for i in range(4)]
        shifts = [table[0, out] for out in outs]
        move_rows(geo, src, (geo.tiles, SPAN), dst, 2 * s, 2 * s + 1, shifts, outs)


class Ring:
    def __init__(self, slots, me, count, device, send, recv):
        self.slots, self.me, self.count, self.device = slots, me, count, device
        self.send, self.recv = send, recv

    def copy(self, k, slot):
        peer = lax.rem(self.me + k, self.count)
        return remote(
            self.slots.at[self.me], self.slots.at[slot], self.send.at[k], self.recv.at[slot], self.device(peer)
        )

    def start(self, value):
        self.slots[pl.ds(self.me, 1)] = value[None]
        for k in range(1, self.count):
            self.copy(k, self.me).start()

    def total(self):
        for k in range(1, self.count):
            source = lax.rem(self.me + k, self.count)
            self.copy(k, source).wait_recv()
        return jnp.sum(self.slots[...], axis=0)

    def sent(self):
        for k in range(1, self.count):
            self.copy(k, self.me).wait_send()


def along(values, index, axis):
    numbers = lax.GatherDimensionNumbers(
        offset_dims=(),
        collapsed_slice_dims=(axis,),
        start_index_map=(axis,),
        operand_batching_dims=(1 - axis,),
        start_indices_batching_dims=(1 - axis,),
    )
    return lax.gather(
        values, index[..., None], numbers, slice_sizes=(1, 1), mode=lax.GatherScatterMode.PROMISE_IN_BOUNDS
    )


def kernel(
    geo,
    spectra_ref,
    mask_hbm,
    delay_hbm,
    out_ref,
    x,
    gram,
    stat_y,
    stat_z,
    power_y,
    power_z,
    table_v,
    table,
    thin,
    plane,
    left,
    right,
    final,
    coded,
    got,
    best,
    mask_ref,
    delay_ref,
    load_sem,
    small_sem,
    table_sem,
    halo_send,
    halo_recv,
    ring_send,
    ring_recv,
    swap_send,
    swap_recv,
    own_sem,
):
    tiles, own = geo.tiles, geo.own
    sub_index = lax.axis_index("sub")
    tm_index = lax.axis_index("tm")
    z_index, y_index = tm_index // geo.ny, lax.rem(tm_index, geo.ny)
    position = reversed_bits(sub_index, 3)
    n_tm = geo.ny * geo.nz
    not_first = tm_index > 0
    not_last = tm_index < n_tm - 1
    lane = iota((8, LANES), 1)
    place = iota((8, LANES), 0)

    def along_y(peer):
        return {"tm": z_index * geo.ny + peer}

    def along_z(peer):
        return {"tm": peer * geo.ny + y_index}

    barrier = pltpu.get_barrier_semaphore()
    for k in range(1, geo.ny):
        pl.semaphore_signal(barrier, inc=1, device_id=along_y(lax.rem(y_index + k, geo.ny)), device_id_type=MESH)
    for k in range(1, geo.nz):
        pl.semaphore_signal(barrier, inc=1, device_id=along_z(lax.rem(z_index + k, geo.nz)), device_id_type=MESH)
    for k in range(1, geo.n_sub):
        pl.semaphore_signal(
            barrier, inc=1, device_id={"sub": lax.rem(sub_index + k, geo.n_sub)}, device_id_type=MESH
        )
    for k in (1, n_tm - 1):
        pl.semaphore_signal(barrier, inc=1, device_id={"tm": lax.rem(tm_index + k, n_tm)}, device_id_type=MESH)

    own_first = LEFT * LANES
    right_first = (LEFT + own) * LANES
    chunk = geo.samples // 4
    loads = []
    for i in range(4):
        loads.append(
            pltpu.make_async_copy(
                spectra_ref.at[:, pl.ds(i * chunk, chunk)],
                x.at[:, pl.ds(own_first + i * chunk, chunk)],
                load_sem.at[i],
            )
        )
        loads[-1].start()
    small = [
        pltpu.make_async_copy(mask_hbm, mask_ref, small_sem.at[0]),
        pltpu.make_async_copy(delay_hbm, delay_ref, small_sem.at[1]),
    ]
    for copy in small:
        copy.start()

    sums = jnp.zeros((8, geo.channels), F32)
    nt = (((1,), (1,)), ((), ()))
    for i in range(4):
        loads[i].wait()
        part = x[:, pl.ds(own_first + i * chunk, chunk)]
        square = lax.dot_general(part, part, nt, preferred_element_type=F32)
        if i == 0:
            gram[...] = square
        else:
            gram[...] += square
        sums = sums + lax.dot_general(jnp.ones((8, chunk), BF16), part, nt, preferred_element_type=F32)
    diagonal = iota((geo.channels, geo.channels), 0) == iota((geo.channels, geo.channels), 1)
    squares = jnp.sum(jnp.where(diagonal, gram[...], 0.0), axis=0, keepdims=True)
    half = geo.channels // 2
    stats = jnp.concatenate(
        [sums[0:1, :half], sums[0:1, half:], squares[:, :half], squares[:, half:]], axis=0
    )
    pl.semaphore_wait(barrier, geo.ny + geo.nz + geo.n_sub - 1)
    over_y = Ring(stat_y, y_index, geo.ny, along_y, ring_send.at[0], ring_recv.at[0])
    over_z = Ring(stat_z, z_index, geo.nz, along_z, ring_send.at[1], ring_recv.at[1])
    over_y.start(stats)

    def to_prev():
        return remote(
            spectra_ref.at[:, pl.ds(0, RIGHT * LANES)],
            x.at[:, pl.ds(right_first, RIGHT * LANES)],
            halo_send.at[0],
            halo_recv.at[0],
            {"tm": tm_index - 1},
        )

    def to_next():
        return remote(
            spectra_ref.at[:, pl.ds(geo.samples - LEFT * LANES, LEFT * LANES)],
            x.at[:, pl.ds(0, LEFT * LANES)],
            halo_send.at[1],
            halo_recv.at[1],
            {"tm": tm_index + 1},
        )

    @pl.when(not_first)
    def _():
        to_prev().start()

    @pl.when(not_last)
    def _():
        to_next().start()

    @pl.when(jnp.logical_not(not_first))
    def _():
        x[:, pl.ds(0, LEFT * LANES)] = jnp.zeros((geo.channels, LEFT * LANES), BF16)

    @pl.when(jnp.logical_not(not_last))
    def _():
        x[:, pl.ds(right_first, RIGHT * LANES)] = jnp.zeros((geo.channels, RIGHT * LANES), BF16)

    for copy in small:
        copy.wait()
    table_v[...] = delay_table(geo, position, sub_index, delay_ref)
    table_copy = pltpu.make_async_copy(table_v, table, table_sem)
    table_copy.start()
    over_z.start(over_y.total())

    totals = over_z.total()
    table_copy.wait()
    total_time = geo.samples * n_tm
    centre = jnp.concatenate([totals[0:1], totals[1:2]], axis=1) / total_time
    power = jnp.concatenate([totals[2:3], totals[3:4]], axis=1) / total_time
    spread = lax.rsqrt(power - centre * centre + 1e-05)
    weight = spread * mask_ref[...].astype(F32)
    bands = geo.channels // 8
    member = iota((bands, geo.channels), 1) // 8 == iota((bands, geo.channels), 0)
    gain = jnp.where(member, weight, 0.0)
    gain_1 = gain.astype(BF16)
    rest = gain - gain_1.astype(F32)
    gain_2 = rest.astype(BF16)
    gain_3 = (rest - gain_2.astype(F32)).astype(BF16)
    gains = jnp.concatenate([gain_1, gain_2, gain_3], axis=0)
    offset = -jnp.sum(gain * centre, axis=1, keepdims=True)

    def normalise(first, count, shift):
        sample = jnp.dot(gains, x[:, pl.ds(first * LANES, count * LANES)], preferred_element_type=F32)
        value = sample[:bands] + sample[bands : 2 * bands] + sample[2 * bands :] + shift
        for g in range(bands // 8):
            for j in range(count):
                thin[pl.ds(8 * g * tiles + first + j, 8, stride=tiles), :] = value[
                    8 * g : 8 * g + 8, j * LANES : (j + 1) * LANES
                ]

    for i in range(own // 4):
        normalise(LEFT + 4 * i, 4, offset)

    @pl.when(not_first)
    def _():
        to_prev().wait_send()
        to_next().wait_recv()

    @pl.when(not_last)
    def _():
        to_next().wait_send()
        to_prev().wait_recv()

    normalise(0, LEFT, jnp.where(not_first, offset, 0.0))
    normalise(LEFT + own, RIGHT, jnp.where(not_last, offset, 0.0))

    first_merge(geo, thin, plane, table)
    pairs = SPAN // 2

    def swap(k, peer, slot):
        return remote(coded.at[peer], got.at[slot], swap_send.at[k], swap_recv.at[slot], {"sub": peer})

    keep = pltpu.make_async_copy(coded.at[sub_index], got.at[position], own_sem)

    def piece(block, j):
        return pl.ds(pl.multiple_of(8 * (block * SPAN + j), 8), 8)

    def column(j):
        return slice(j * LANES, (j + 1) * LANES)

    def encode(peer):
        powers = jnp.zeros((8, LANES), F32)
        for j in range(pairs):
            one = right[piece(peer, j), :]
            two = right[piece(peer, j + pairs), :]
            largest = jnp.max(jnp.maximum(jnp.abs(one), jnp.abs(two)), axis=1, keepdims=True)
            power = jnp.ceil(jnp.log2(jnp.maximum(largest, 1e-30) * 1.001))
            factor = jnp.exp2(15.0 - power)
            code = jnp.concatenate([one * factor, two * factor], axis=0)
            coded[pl.ds(peer, 1), :, column(j)] = jnp.round(code).astype(I32).astype(jnp.int16)[None]
            powers = jnp.where(lane == j, power, powers)
        powers = jnp.concatenate([powers, powers], axis=0)
        coded[pl.ds(peer, 1), :, column(pairs)] = powers.astype(I32).astype(jnp.int16)[None]

    near = sub_index // 4
    far = 1 - near
    place_in_half = lax.rem(sub_index, 4)
    for half, first in ((far, 0), (near, 4)):
        merge(geo, plane, left, table, 5, 4, half)
        merge(geo, left, right, table, 6, 8, half)
        merge(geo, right, left, table, 7, 16, half)
        merge(geo, left, right, table, 8, 32, half)

        def send(k, carry):
            peer = 4 * half + lax.rem(place_in_half + k, 4)
            encode(peer)
            if first == 0:
                swap(first + k, peer, position).start()
            else:

                @pl.when(k < 4)
                def _():
                    swap(first + k, peer, position).start()

                @pl.when(k == 4)
                def _():
                    keep.start()

            return carry

        if first == 0:
            lax.fori_loop(0, 4, send, 0)
        else:
            lax.fori_loop(1, 5, send, 0)

    def decode(slot):
        block = got[pl.ds(slot, 1), :, column(pairs)]
        scales = jnp.exp2(jnp.reshape(block, (16, LANES)).astype(F32)[0:8] - 15.0)
        for j in range(pairs):
            code = jnp.reshape(got[pl.ds(slot, 1), :, column(j)], (16, LANES)).astype(F32)
            scale = along(scales, jnp.full((8, LANES), j, I32), 1)
            plane[piece(slot, j), :] = code[0:8] * scale
            plane[piece(slot, j + pairs), :] = code[8:16] * scale

    keep.wait()
    decode(position)

    def receive(source):
        slot = reversed_bits(source, 3)
        swap(0, source, slot).wait_recv()
        decode(slot)

    def receive_far(k, carry):
        receive(4 * far + lax.rem(place_in_half + 4 - k, 4))
        return carry

    def receive_near(k, carry):
        receive(4 * near + lax.rem(place_in_half + 4 - k, 4))
        return carry

    lax.fori_loop(0, 4, receive_far, 0)
    lax.fori_loop(1, 4, receive_near, 0)

    merge(geo, plane, left, table, 9, 8)
    merge(geo, left, right, table, 10, 16)
    merge(geo, right, final, table, 11, 32, to_step=tiles)

    def group_tile(g, j):
        return final[pl.ds(8 * g * tiles + j, 8, stride=tiles), :]

    def group_power(g, packed):
        total = jnp.zeros((8, LANES), F32)
        for j in range(LEFT, LEFT + own):
            tile = group_tile(g, j)
            total = total + tile * tile
        return jnp.where(lane == 8 * g + place, jnp.sum(total, axis=1, keepdims=True), packed)

    packed = lax.fori_loop(0, 8, group_power, jnp.zeros((8, LANES), F32), unroll=8)
    rings = [over_y, over_z]
    over_y = Ring(power_y, y_index, geo.ny, along_y, ring_send.at[2], ring_recv.at[2])
    over_z = Ring(power_z, z_index, geo.nz, along_z, ring_send.at[3], ring_recv.at[3])
    over_y.start(jnp.sum(packed, axis=0, keepdims=True))

    def group_best(g, carry):
        box = [jnp.where(not_first, group_tile(g, 0), 0.0)]
        box += [group_tile(g, j) for j in range(1, LEFT + own)]
        kept = jnp.zeros((8, LANES), F32)
        for section in range(WIDTHS):
            if section > 0:
                lag = 2 ** (section - 1)
                near = lane < LANES - lag
                for j in range(LEFT + own - 1, -1, -1):
                    mixed = jnp.where(near, box[j], box[max(j - 1, 0)])
                    box[j] = box[j] + pltpu.roll(mixed, lag, 1)
            found = [jnp.maximum(box[LEFT + 2 * b], box[LEFT + 2 * b + 1]) for b in range(own // 2)]
            step = 1
            while len(found) > 1:
                even = (lane & step) == 0
                found = [
                    jnp.maximum(jnp.where(even, a, b), pltpu.roll(jnp.where(even, b, a), step, 1))
                    for a, b in zip(found[::2], found[1::2])
                ]
                step *= 2
            largest = found[0]
            while step < LANES:
                largest = jnp.maximum(largest, pltpu.roll(largest, step, 1))
                step *= 2
            kept = jnp.where((lane >> 4) == section, largest * (1.0 / math.sqrt(2**section)), kept)
        best[pl.ds(pl.multiple_of(8 * g, 8), 8), :] = kept
        return carry

    lax.fori_loop(0, 4, group_best, 0, unroll=2)
    over_z.start(over_y.total())
    lax.fori_loop(4, 8, group_best, 0, unroll=2)
    for k in (0, 1, 2, 3, 5, 6, 7):
        swap(k, 4 * (far if k < 4 else near) + lax.rem(place_in_half + k, 4), position).wait_send()
    mean_power = over_z.total() / total_time
    for ring in rings + [over_y, over_z]:
        ring.sent()
    inverse = jnp.broadcast_to(1.0 / jnp.sqrt(mean_power + 1e-06), (8, LANES))
    for g in range(8):
        scale = jnp.sum(jnp.where(lane == 8 * g + place, inverse, 0.0), axis=1, keepdims=True)
        best[8 * g : 8 * g + 8, :] = best[8 * g : 8 * g + 8, :] * scale
    out_ref[...] = best[...].T


class Geometry:
    pass


def local(mesh, spectra, chan_mask, delay_step):
    geo = Geometry()
    geo.n_sub = mesh.shape["sub"]
    n_tm = mesh.shape["tm"]
    geo.ny = 4
    geo.nz = n_tm // geo.ny
    geo.channels, geo.samples = spectra.shape
    geo.own = geo.samples // LANES
    geo.tiles = LEFT + geo.own + RIGHT
    assert (geo.n_sub, geo.channels, geo.own, geo.ny * geo.nz) == (8, 256, 32, n_tm)
    dma = pltpu.SemaphoreType.DMA
    slots = max(geo.ny, geo.nz)
    width = geo.tiles * LANES
    geo.rows, geo.local_levels, geo.cross_levels = 64, 8, 3
    anywhere = pl.BlockSpec(memory_space=pl.ANY)
    best = pl.pallas_call(
        functools.partial(kernel, geo),
        out_shape=jax.ShapeDtypeStruct((WIDTHS * geo.own // 2, 64), F32),
        in_specs=[anywhere, anywhere, anywhere],
        out_specs=pl.BlockSpec(memory_space=pltpu.VMEM),
        scratch_shapes=[
            pltpu.VMEM((geo.channels, width), BF16),
            pltpu.VMEM((geo.channels, geo.channels), F32),
            pltpu.VMEM((geo.ny, 4, LANES), F32),
            pltpu.VMEM((geo.nz, 4, LANES), F32),
            pltpu.VMEM((geo.ny, 1, LANES), F32),
            pltpu.VMEM((geo.nz, 1, LANES), F32),
            pltpu.VMEM((8, LANES), I32),
            pltpu.SMEM((8, LANES), I32),
            pltpu.VMEM((32 * geo.tiles + 64, LANES), F32),
            pltpu.VMEM((64 * SPAN + 16, LANES), F32),
            pltpu.VMEM((64 * SPAN + 16, LANES), F32),
            pltpu.VMEM((64 * SPAN + 16, LANES), F32),
            pltpu.VMEM((64 * geo.tiles + 64, LANES), F32),
            pltpu.VMEM((8, 16, (SPAN // 2 + 1) * LANES), jnp.int16),
            pltpu.VMEM((8, 16, (SPAN // 2 + 1) * LANES), jnp.int16),
            pltpu.VMEM((64, LANES), F32),
            pltpu.VMEM((1, geo.channels), I32),
            pltpu.VMEM((16, LANES), I32),
            dma((4,)),
            dma((2,)),
            dma(()),
            dma((2,)),
            dma((2,)),
            dma((4, slots)),
            dma((4, slots)),
            dma((geo.n_sub,)),
            dma((geo.n_sub,)),
            dma(()),
        ],
        compiler_params=pltpu.CompilerParams(collective_id=0, has_side_effects=True, vmem_limit_bytes=62 * 2**20),
        name="dedisperse",
    )(spectra, chan_mask.reshape(1, geo.channels), delay_step.reshape(16, LANES))
    return best.reshape(WIDTHS, geo.own // 2, 64).transpose(2, 0, 1)


def solution(mesh):
    in_specs = (P("sub", "tm"), P("sub"), P())
    out_specs = P("sub", None, "tm")
    return jax.shard_map(
        functools.partial(local, mesh), mesh=mesh, in_specs=in_specs, out_specs=out_specs, check_vma=False
    )
```

```python
import functools
import math

import jax
import jax.numpy as jnp
from jax import lax
from jax.experimental import pallas as pl
from jax.experimental.pallas import tpu as pltpu
from jax.sharding import PartitionSpec as P

MESH = pl.DeviceIdType.MESH
F32 = jnp.float32
BF16 = jnp.bfloat16
I32 = jnp.int32

WIDTHS = 8
LANES = 128
LEFT = 1
RIGHT = 4
SPAN = 40


def reversed_bits(number, bit_count):
    result = 0
    for place in range(bit_count):
        result = result + ((number >> place) % 2) * 2 ** (bit_count - 1 - place)
    return result


def iota(shape, dim):
    return lax.broadcasted_iota(I32, shape, dim)


def remote(src, dst, send_sem, recv_sem, device_id):
    return pltpu.make_async_remote_copy(
        src_ref=src,
        dst_ref=dst,
        send_sem=send_sem,
        recv_sem=recv_sem,
        device_id=device_id,
        device_id_type=MESH,
    )


def delay_table(geo, position, sub_index, delay_ref):
    rows = geo.rows
    level_rows = []
    local = delay_ref[pl.ds(2 * position, 2), :].astype(F32)
    local = jnp.concatenate([local[0:1], local[1:2]], axis=1)
    local = jnp.broadcast_to(local, (8, geo.channels)).astype(BF16)
    channel = iota((rows, geo.channels), 1)
    row = iota((rows, geo.channels), 0)
    blocks = jnp.sum(delay_ref[...].astype(F32), axis=1, keepdims=True)
    block = iota((2 * geo.n_sub, rows), 0) // 2
    lane_row = iota((1, rows), 1)
    for level in range(4, geo.local_levels + geo.cross_levels + 1):
        if level <= geo.local_levels:
            depth = level - 2
            band = row >> depth
            spans = []
            for mask in ((channel >> (level - 1)) == 2 * band, (channel >> level) == band):
                spans.append(
                    lax.dot_general(
                        local, mask.astype(F32).astype(BF16), (((1,), (1,)), ((), ())), preferred_element_type=F32
                    )[0:1]
                )
            trial = lane_row & (2**depth - 1)
        else:
            depth = level - 2 - geo.cross_levels
            band = iota((2 * geo.n_sub, rows), 1) >> depth
            up = level - geo.local_levels
            spans = []
            for mask in ((block >> (up - 1)) == 2 * band, (block >> up) == band):
                spans.append(jnp.sum(jnp.where(mask, blocks, 0.0), axis=0, keepdims=True))
            trial = sub_index * 2**depth + (lane_row & (2**depth - 1))
        early = spans[0].astype(I32)
        whole = jnp.maximum(spans[1].astype(I32), 1)
        product = trial * early
        shift = (product.astype(F32) / whole.astype(F32)).astype(I32)
        rest = product - shift * whole
        shift = shift + jnp.where(rest >= whole, 1, 0) - jnp.where(rest < 0, 1, 0)
        level_rows.append(jnp.clip(shift, 0, 2 ** (level - 3) - 1))
    table = jnp.concatenate(level_rows, axis=0)
    return jnp.concatenate([table, table], axis=1)


def move_rows(geo, src, steps, dst, lower, upper, shifts, outs, wide=False):
    lane = iota((SPAN, LANES), 1)
    from_step, to_step = steps
    lower_rows = src[pl.ds(lower * from_step, SPAN), :]
    start = upper * from_step
    if not wide:
        here = src[pl.ds(start, SPAN), :]
        after = src[pl.ds(start + 1, SPAN), :]
    for shift, out in zip(shifts, outs):
        if wide:
            tile = start + (shift >> 7)
            shift = shift & (LANES - 1)
            here = src[pl.ds(tile, SPAN), :]
            after = src[pl.ds(tile + 1, SPAN), :]
        mixed = jnp.where(lane >= shift, here, after)
        dst[pl.ds(out * to_step, SPAN), :] = lower_rows + pltpu.roll(mixed, (LANES - shift) & (LANES - 1), 1)


def merge(geo, src, dst, table, level, fan, half=None, to_step=SPAN):
    for s in range(32 // fan):
        for e in range(fan if half is None else fan // 2):
            first = e if half is None else half * (fan // 2) + e
            p = s * fan + first
            outs = [2 * p, 2 * p + 1]
            shifts = [table[level - 4, out] for out in outs]
            low = s * 2 * fan + first
            move_rows(geo, src, (SPAN, to_step), dst, low, low + fan, shifts, outs, wide=level == 11)


def first_merge(geo, src, dst, table):
    for s in range(16):
        outs = [4 * s + i for i in range(4)]
        shifts = [table[0, out] for out in outs]
        move_rows(geo, src, (geo.tiles, SPAN), dst, 2 * s, 2 * s + 1, shifts, outs)


class Ring:
    def __init__(self, slots, me, count, device, send, recv):
        self.slots, self.me, self.count, self.device = slots, me, count, device
        self.send, self.recv = send, recv

    def copy(self, k, slot):
        peer = lax.rem(self.me + k, self.count)
        return remote(
            self.slots.at[self.me], self.slots.at[slot], self.send.at[k], self.recv.at[slot], self.device(peer)
        )

    def start(self, value):
        self.slots[pl.ds(self.me, 1)] = value[None]
        for k in range(1, self.count):
            self.copy(k, self.me).start()

    def total(self):
        for k in range(1, self.count):
            source = lax.rem(self.me + k, self.count)
            self.copy(k, source).wait_recv()
        return jnp.sum(self.slots[...], axis=0)

    def sent(self):
        for k in range(1, self.count):
            self.copy(k, self.me).wait_send()


def along(values, index, axis):
    numbers = lax.GatherDimensionNumbers(
        offset_dims=(),
        collapsed_slice_dims=(axis,),
        start_index_map=(axis,),
        operand_batching_dims=(1 - axis,),
        start_indices_batching_dims=(1 - axis,),
    )
    return lax.gather(
        values, index[..., None], numbers, slice_sizes=(1, 1), mode=lax.GatherScatterMode.PROMISE_IN_BOUNDS
    )


def kernel(
    geo,
    spectra_ref,
    mask_hbm,
    delay_hbm,
    out_ref,
    x,
    gram,
    stat_y,
    stat_z,
    power_y,
    power_z,
    table_v,
    table,
    thin,
    plane,
    left,
    right,
    final,
    coded,
    got,
    best,
    mask_ref,
    delay_ref,
    load_sem,
    small_sem,
    table_sem,
    halo_send,
    halo_recv,
    ring_send,
    ring_recv,
    swap_send,
    swap_recv,
    own_sem,
):
    tiles, own = geo.tiles, geo.own
    sub_index = lax.axis_index("sub")
    tm_index = lax.axis_index("tm")
    z_index, y_index = tm_index // geo.ny, lax.rem(tm_index, geo.ny)
    position = reversed_bits(sub_index, 3)
    n_tm = geo.ny * geo.nz
    not_first = tm_index > 0
    not_last = tm_index < n_tm - 1
    lane = iota((8, LANES), 1)
    place = iota((8, LANES), 0)

    def along_y(peer):
        return {"tm": z_index * geo.ny + peer}

    def along_z(peer):
        return {"tm": peer * geo.ny + y_index}

    barrier = pltpu.get_barrier_semaphore()
    for k in range(1, geo.ny):
        pl.semaphore_signal(barrier, inc=1, device_id=along_y(lax.rem(y_index + k, geo.ny)), device_id_type=MESH)
    for k in range(1, geo.nz):
        pl.semaphore_signal(barrier, inc=1, device_id=along_z(lax.rem(z_index + k, geo.nz)), device_id_type=MESH)
    for k in range(1, geo.n_sub):
        pl.semaphore_signal(
            barrier, inc=1, device_id={"sub": lax.rem(sub_index + k, geo.n_sub)}, device_id_type=MESH
        )
    for k in (1, n_tm - 1):
        pl.semaphore_signal(barrier, inc=1, device_id={"tm": lax.rem(tm_index + k, n_tm)}, device_id_type=MESH)

    own_first = LEFT * LANES
    right_first = (LEFT + own) * LANES
    chunk = geo.samples // 4
    loads = []
    for i in range(4):
        loads.append(
            pltpu.make_async_copy(
                spectra_ref.at[:, pl.ds(i * chunk, chunk)],
                x.at[:, pl.ds(own_first + i * chunk, chunk)],
                load_sem.at[i],
            )
        )
        loads[-1].start()
    small = [
        pltpu.make_async_copy(mask_hbm, mask_ref, small_sem.at[0]),
        pltpu.make_async_copy(delay_hbm, delay_ref, small_sem.at[1]),
    ]
    for copy in small:
        copy.start()

    sums = jnp.zeros((8, geo.channels), F32)
    nt = (((1,), (1,)), ((), ()))
    for i in range(4):
        loads[i].wait()
        part = x[:, pl.ds(own_first + i * chunk, chunk)]
        square = lax.dot_general(part, part, nt, preferred_element_type=F32)
        if i == 0:
            gram[...] = square
        else:
            gram[...] += square
        sums = sums + lax.dot_general(jnp.ones((8, chunk), BF16), part, nt, preferred_element_type=F32)
    diagonal = iota((geo.channels, geo.channels), 0) == iota((geo.channels, geo.channels), 1)
    squares = jnp.sum(jnp.where(diagonal, gram[...], 0.0), axis=0, keepdims=True)
    half = geo.channels // 2
    stats = jnp.concatenate(
        [sums[0:1, :half], sums[0:1, half:], squares[:, :half], squares[:, half:]], axis=0
    )
    pl.semaphore_wait(barrier, geo.ny + geo.nz + geo.n_sub - 1)
    over_y = Ring(stat_y, y_index, geo.ny, along_y, ring_send.at[0], ring_recv.at[0])
    over_z = Ring(stat_z, z_index, geo.nz, along_z, ring_send.at[1], ring_recv.at[1])
    over_y.start(stats)

    def to_prev():
        return remote(
            spectra_ref.at[:, pl.ds(0, RIGHT * LANES)],
            x.at[:, pl.ds(right_first, RIGHT * LANES)],
            halo_send.at[0],
            halo_recv.at[0],
            {"tm": tm_index - 1},
        )

    def to_next():
        return remote(
            spectra_ref.at[:, pl.ds(geo.samples - LEFT * LANES, LEFT * LANES)],
            x.at[:, pl.ds(0, LEFT * LANES)],
            halo_send.at[1],
            halo_recv.at[1],
            {"tm": tm_index + 1},
        )

    @pl.when(not_first)
    def _():
        to_prev().start()

    @pl.when(not_last)
    def _():
        to_next().start()

    @pl.when(jnp.logical_not(not_first))
    def _():
        x[:, pl.ds(0, LEFT * LANES)] = jnp.zeros((geo.channels, LEFT * LANES), BF16)

    @pl.when(jnp.logical_not(not_last))
    def _():
        x[:, pl.ds(right_first, RIGHT * LANES)] = jnp.zeros((geo.channels, RIGHT * LANES), BF16)

    thin[pl.ds(32 * tiles, 64), :] = jnp.zeros((64, LANES), F32)

    for copy in small:
        copy.wait()
    table_v[...] = delay_table(geo, position, sub_index, delay_ref)
    table_copy = pltpu.make_async_copy(table_v, table, table_sem)
    table_copy.start()
    over_z.start(over_y.total())

    totals = over_z.total()
    table_copy.wait()
    total_time = geo.samples * n_tm
    centre = jnp.concatenate([totals[0:1], totals[1:2]], axis=1) / total_time
    power = jnp.concatenate([totals[2:3], totals[3:4]], axis=1) / total_time
    spread = lax.rsqrt(power - centre * centre + 1e-05)
    weight = spread * mask_ref[...].astype(F32)
    bands = geo.channels // 8
    member = iota((bands, geo.channels), 1) // 8 == iota((bands, geo.channels), 0)
    gain = jnp.where(member, weight, 0.0)
    gain_1 = gain.astype(BF16)
    rest = gain - gain_1.astype(F32)
    gain_2 = rest.astype(BF16)
    gain_3 = (rest - gain_2.astype(F32)).astype(BF16)
    gains = jnp.concatenate([gain_1, gain_2, gain_3], axis=0)
    offset = -jnp.sum(gain * centre, axis=1, keepdims=True)

    def normalise(first, count, shift):
        sample = jnp.dot(gains, x[:, pl.ds(first * LANES, count * LANES)], preferred_element_type=F32)
        value = sample[:bands] + sample[bands : 2 * bands] + sample[2 * bands :] + shift
        for g in range(bands // 8):
            for j in range(count):
                thin[pl.ds(8 * g * tiles + first + j, 8, stride=tiles), :] = value[
                    8 * g : 8 * g + 8, j * LANES : (j + 1) * LANES
                ]

    for i in range(own // 4):
        normalise(LEFT + 4 * i, 4, offset)

    @pl.when(not_first)
    def _():
        to_prev().wait_send()
        to_next().wait_recv()

    @pl.when(not_last)
    def _():
        to_next().wait_send()
        to_prev().wait_recv()

    normalise(0, LEFT, jnp.where(not_first, offset, 0.0))
    normalise(LEFT + own, RIGHT, jnp.where(not_last, offset, 0.0))

    first_merge(geo, thin, plane, table)
    pairs = SPAN // 2

    def swap(k, peer, slot):
        return remote(coded.at[peer], got.at[slot], swap_send.at[k], swap_recv.at[slot], {"sub": peer})

    keep = pltpu.make_async_copy(coded.at[sub_index], got.at[position], own_sem)

    def piece(block, j):
        return pl.ds(pl.multiple_of(8 * (block * SPAN + j), 8), 8)

    def column(j):
        return slice(j * LANES, (j + 1) * LANES)

    def encode(peer):
        powers = jnp.zeros((8, LANES), F32)
        for j in range(pairs):
            one = right[piece(peer, j), :]
            two = right[piece(peer, j + pairs), :]
            largest = jnp.max(jnp.maximum(jnp.abs(one), jnp.abs(two)), axis=1, keepdims=True)
            power = jnp.ceil(jnp.log2(jnp.maximum(largest, 1e-30) * 1.001))
            factor = jnp.exp2(15.0 - power)
            code = jnp.concatenate([one * factor, two * factor], axis=0)
            coded[pl.ds(peer, 1), :, column(j)] = jnp.round(code).astype(I32).astype(jnp.int16)[None]
            powers = jnp.where(lane == j, power, powers)
        powers = jnp.concatenate([powers, powers], axis=0)
        coded[pl.ds(peer, 1), :, column(pairs)] = powers.astype(I32).astype(jnp.int16)[None]

    near = sub_index // 4
    far = 1 - near
    place_in_half = lax.rem(sub_index, 4)
    for half, first in ((far, 0), (near, 4)):
        merge(geo, plane, left, table, 5, 4, half)
        merge(geo, left, right, table, 6, 8, half)
        merge(geo, right, left, table, 7, 16, half)
        merge(geo, left, right, table, 8, 32, half)

        def send(k, carry):
            peer = 4 * half + lax.rem(place_in_half + k, 4)
            encode(peer)
            if first == 0:
                swap(first + k, peer, position).start()
            else:

                @pl.when(k < 4)
                def _():
                    swap(first + k, peer, position).start()

                @pl.when(k == 4)
                def _():
                    keep.start()

            return carry

        if first == 0:
            lax.fori_loop(0, 4, send, 0)
        else:
            lax.fori_loop(1, 5, send, 0)

    def decode(slot):
        block = got[pl.ds(slot, 1), :, column(pairs)]
        scales = jnp.exp2(jnp.reshape(block, (16, LANES)).astype(F32)[0:8] - 15.0)
        for j in range(pairs):
            code = jnp.reshape(got[pl.ds(slot, 1), :, column(j)], (16, LANES)).astype(F32)
            scale = along(scales, jnp.full((8, LANES), j, I32), 1)
            plane[piece(slot, j), :] = code[0:8] * scale
            plane[piece(slot, j + pairs), :] = code[8:16] * scale

    keep.wait()
    decode(position)

    def receive(source):
        slot = reversed_bits(source, 3)
        swap(0, source, slot).wait_recv()
        decode(slot)

    def receive_far(k, carry):
        receive(4 * far + lax.rem(place_in_half + 4 - k, 4))
        return carry

    def receive_near(k, carry):
        receive(4 * near + lax.rem(place_in_half + 4 - k, 4))
        return carry

    lax.fori_loop(0, 4, receive_far, 0)
    lax.fori_loop(1, 4, receive_near, 0)

    merge(geo, plane, left, table, 9, 8)
    merge(geo, left, right, table, 10, 16)
    merge(geo, right, final, table, 11, 32, to_step=tiles)

    def group_tile(g, j):
        return final[pl.ds(8 * g * tiles + j, 8, stride=tiles), :]

    def group_power(g, packed):
        total = jnp.zeros((8, LANES), F32)
        for j in range(LEFT, LEFT + own):
            tile = group_tile(g, j)
            total = total + tile * tile
        return jnp.where(lane == 8 * g + place, jnp.sum(total, axis=1, keepdims=True), packed)

    packed = lax.fori_loop(0, 8, group_power, jnp.zeros((8, LANES), F32), unroll=8)
    rings = [over_y, over_z]
    over_y = Ring(power_y, y_index, geo.ny, along_y, ring_send.at[2], ring_recv.at[2])
    over_z = Ring(power_z, z_index, geo.nz, along_z, ring_send.at[3], ring_recv.at[3])
    over_y.start(jnp.sum(packed, axis=0, keepdims=True))

    def group_best(g, carry):
        box = [jnp.where(not_first, group_tile(g, 0), 0.0)]
        box += [group_tile(g, j) for j in range(1, LEFT + own)]
        kept = jnp.zeros((8, LANES), F32)
        for section in range(WIDTHS):
            if section > 0:
                lag = 2 ** (section - 1)
                near = lane < LANES - lag
                for j in range(LEFT + own - 1, -1, -1):
                    mixed = jnp.where(near, box[j], box[max(j - 1, 0)])
                    box[j] = box[j] + pltpu.roll(mixed, lag, 1)
            found = [jnp.maximum(box[LEFT + 2 * b], box[LEFT + 2 * b + 1]) for b in range(own // 2)]
            step = 1
            while len(found) > 1:
                even = (lane & step) == 0
                found = [
                    jnp.maximum(jnp.where(even, a, b), pltpu.roll(jnp.where(even, b, a), step, 1))
                    for a, b in zip(found[::2], found[1::2])
                ]
                step *= 2
            largest = found[0]
            while step < LANES:
                largest = jnp.maximum(largest, pltpu.roll(largest, step, 1))
                step *= 2
            kept = jnp.where((lane >> 4) == section, largest * (1.0 / math.sqrt(2**section)), kept)
        best[pl.ds(pl.multiple_of(8 * g, 8), 8), :] = kept
        return carry

    lax.fori_loop(0, 4, group_best, 0, unroll=2)
    over_z.start(over_y.total())
    lax.fori_loop(4, 8, group_best, 0, unroll=2)
    for k in (0, 1, 2, 3, 5, 6, 7):
        swap(k, 4 * (far if k < 4 else near) + lax.rem(place_in_half + k, 4), position).wait_send()
    mean_power = over_z.total() / total_time
    for ring in rings + [over_y, over_z]:
        ring.sent()
    inverse = jnp.broadcast_to(1.0 / jnp.sqrt(mean_power + 1e-06), (8, LANES))
    for g in range(8):
        scale = jnp.sum(jnp.where(lane == 8 * g + place, inverse, 0.0), axis=1, keepdims=True)
        best[8 * g : 8 * g + 8, :] = best[8 * g : 8 * g + 8, :] * scale
    out_ref[...] = best[...].T


class Geometry:
    pass


def local(mesh, spectra, chan_mask, delay_step):
    geo = Geometry()
    geo.n_sub = mesh.shape["sub"]
    n_tm = mesh.shape["tm"]
    geo.ny = 4
    geo.nz = n_tm // geo.ny
    geo.channels, geo.samples = spectra.shape
    geo.own = geo.samples // LANES
    geo.tiles = LEFT + geo.own + RIGHT
    assert (geo.n_sub, geo.channels, geo.own, geo.ny * geo.nz) == (8, 256, 32, n_tm)
    dma = pltpu.SemaphoreType.DMA
    slots = max(geo.ny, geo.nz)
    width = geo.tiles * LANES
    geo.rows, geo.local_levels, geo.cross_levels = 64, 8, 3
    anywhere = pl.BlockSpec(memory_space=pl.ANY)
    best = pl.pallas_call(
        functools.partial(kernel, geo),
        out_shape=jax.ShapeDtypeStruct((WIDTHS * geo.own // 2, 64), F32),
        in_specs=[anywhere, anywhere, anywhere],
        out_specs=pl.BlockSpec(memory_space=pltpu.VMEM),
        scratch_shapes=[
            pltpu.VMEM((geo.channels, width), BF16),
            pltpu.VMEM((geo.channels, geo.channels), F32),
            pltpu.VMEM((geo.ny, 4, LANES), F32),
            pltpu.VMEM((geo.nz, 4, LANES), F32),
            pltpu.VMEM((geo.ny, 1, LANES), F32),
            pltpu.VMEM((geo.nz, 1, LANES), F32),
            pltpu.VMEM((8, LANES), I32),
            pltpu.SMEM((8, LANES), I32),
            pltpu.VMEM((32 * geo.tiles + 64, LANES), F32),
            pltpu.VMEM((64 * SPAN + 16, LANES), F32),
            pltpu.VMEM((64 * SPAN + 16, LANES), F32),
            pltpu.VMEM((64 * SPAN + 16, LANES), F32),
            pltpu.VMEM((64 * geo.tiles + 64, LANES), F32),
            pltpu.VMEM((8, 16, (SPAN // 2 + 1) * LANES), jnp.int16),
            pltpu.VMEM((8, 16, (SPAN // 2 + 1) * LANES), jnp.int16),
            pltpu.VMEM((64, LANES), F32),
            pltpu.VMEM((1, geo.channels), I32),
            pltpu.VMEM((16, LANES), I32),
            dma((4,)),
            dma((2,)),
            dma(()),
            dma((2,)),
            dma((2,)),
            dma((4, slots)),
            dma((4, slots)),
            dma((geo.n_sub,)),
            dma((geo.n_sub,)),
            dma(()),
        ],
        compiler_params=pltpu.CompilerParams(collective_id=0, has_side_effects=True, vmem_limit_bytes=62 * 2**20),
        name="dedisperse",
    )(spectra, chan_mask.reshape(1, geo.channels), delay_step.reshape(16, LANES))
    return best.reshape(WIDTHS, geo.own // 2, 64).transpose(2, 0, 1)


def solution(mesh):
    in_specs = (P("sub", "tm"), P("sub"), P())
    out_specs = P("sub", None, "tm")
    return jax.shard_map(
        functools.partial(local, mesh), mesh=mesh, in_specs=in_specs, out_specs=out_specs, check_vma=False
    )
```

```python
import functools
import math

import jax
import jax.numpy as jnp
from jax import lax
from jax.experimental import pallas as pl
from jax.experimental.pallas import tpu as pltpu
from jax.sharding import PartitionSpec as P

MESH = pl.DeviceIdType.MESH
F32 = jnp.float32
BF16 = jnp.bfloat16
I32 = jnp.int32

WIDTHS = 8
LANES = 128
LEFT = 1
RIGHT = 4
SPAN = 40


def reversed_bits(number, bit_count):
    result = 0
    for place in range(bit_count):
        result = result + ((number >> place) % 2) * 2 ** (bit_count - 1 - place)
    return result


def iota(shape, dim):
    return lax.broadcasted_iota(I32, shape, dim)


def remote(src, dst, send_sem, recv_sem, device_id):
    return pltpu.make_async_remote_copy(
        src_ref=src,
        dst_ref=dst,
        send_sem=send_sem,
        recv_sem=recv_sem,
        device_id=device_id,
        device_id_type=MESH,
    )


def delay_table(geo, position, sub_index, delay_ref):
    rows = geo.rows
    level_rows = []
    local = delay_ref[pl.ds(2 * position, 2), :].astype(F32)
    local = jnp.concatenate([local[0:1], local[1:2]], axis=1)
    local = jnp.broadcast_to(local, (8, geo.channels)).astype(BF16)
    channel = iota((rows, geo.channels), 1)
    row = iota((rows, geo.channels), 0)
    blocks = jnp.sum(delay_ref[...].astype(F32), axis=1, keepdims=True)
    block = iota((2 * geo.n_sub, rows), 0) // 2
    lane_row = iota((1, rows), 1)
    for level in range(4, geo.local_levels + geo.cross_levels + 1):
        if level <= geo.local_levels:
            depth = level - 2
            band = row >> depth
            spans = []
            for mask in ((channel >> (level - 1)) == 2 * band, (channel >> level) == band):
                spans.append(
                    lax.dot_general(
                        local, mask.astype(F32).astype(BF16), (((1,), (1,)), ((), ())), preferred_element_type=F32
                    )[0:1]
                )
            trial = lane_row & (2**depth - 1)
        else:
            depth = level - 2 - geo.cross_levels
            band = iota((2 * geo.n_sub, rows), 1) >> depth
            up = level - geo.local_levels
            spans = []
            for mask in ((block >> (up - 1)) == 2 * band, (block >> up) == band):
                spans.append(jnp.sum(jnp.where(mask, blocks, 0.0), axis=0, keepdims=True))
            trial = sub_index * 2**depth + (lane_row & (2**depth - 1))
        early = spans[0].astype(I32)
        whole = jnp.maximum(spans[1].astype(I32), 1)
        product = trial * early
        shift = (product.astype(F32) / whole.astype(F32)).astype(I32)
        rest = product - shift * whole
        shift = shift + jnp.where(rest >= whole, 1, 0) - jnp.where(rest < 0, 1, 0)
        level_rows.append(jnp.clip(shift, 0, 2 ** (level - 3) - 1))
    table = jnp.concatenate(level_rows, axis=0)
    return jnp.concatenate([table, table], axis=1)


def move_rows(geo, src, steps, dst, lower, upper, shifts, outs, wide=False):
    lane = iota((SPAN, LANES), 1)
    from_step, to_step = steps
    lower_rows = src[pl.ds(lower * from_step, SPAN), :]
    start = upper * from_step
    if not wide:
        here = src[pl.ds(start, SPAN), :]
        after = src[pl.ds(start + 1, SPAN), :]
    for shift, out in zip(shifts, outs):
        if wide:
            tile = start + (shift >> 7)
            shift = shift & (LANES - 1)
            here = src[pl.ds(tile, SPAN), :]
            after = src[pl.ds(tile + 1, SPAN), :]
        mixed = jnp.where(lane >= shift, here, after)
        dst[pl.ds(out * to_step, SPAN), :] = lower_rows + pltpu.roll(mixed, (LANES - shift) & (LANES - 1), 1)


def merge(geo, src, dst, table, level, fan, half=None, to_step=SPAN):
    for s in range(32 // fan):
        for e in range(fan if half is None else fan // 2):
            first = e if half is None else half * (fan // 2) + e
            p = s * fan + first
            outs = [2 * p, 2 * p + 1]
            shifts = [table[level - 4, out] for out in outs]
            low = s * 2 * fan + first
            move_rows(geo, src, (SPAN, to_step), dst, low, low + fan, shifts, outs, wide=level == 11)


def first_merge(geo, src, dst, table):
    for s in range(16):
        outs = [4 * s + i for i in range(4)]
        shifts = [table[0, out] for out in outs]
        move_rows(geo, src, (geo.tiles, SPAN), dst, 2 * s, 2 * s + 1, shifts, outs)


class Ring:
    def __init__(self, slots, me, count, device, send, recv):
        self.slots, self.me, self.count, self.device = slots, me, count, device
        self.send, self.recv = send, recv

    def copy(self, k, slot):
        peer = lax.rem(self.me + k, self.count)
        return remote(
            self.slots.at[self.me], self.slots.at[slot], self.send.at[k], self.recv.at[slot], self.device(peer)
        )

    def start(self, value):
        self.slots[pl.ds(self.me, 1)] = value[None]
        for k in sorted(range(1, self.count), key=lambda k: -min(k, self.count - k)):
            self.copy(k, self.me).start()

    def total(self):
        for k in range(1, self.count):
            source = lax.rem(self.me + k, self.count)
            self.copy(k, source).wait_recv()
        return jnp.sum(self.slots[...], axis=0)

    def sent(self):
        for k in range(1, self.count):
            self.copy(k, self.me).wait_send()


def along(values, index, axis):
    numbers = lax.GatherDimensionNumbers(
        offset_dims=(),
        collapsed_slice_dims=(axis,),
        start_index_map=(axis,),
        operand_batching_dims=(1 - axis,),
        start_indices_batching_dims=(1 - axis,),
    )
    return lax.gather(
        values, index[..., None], numbers, slice_sizes=(1, 1), mode=lax.GatherScatterMode.PROMISE_IN_BOUNDS
    )


def kernel(
    geo,
    spectra_ref,
    mask_hbm,
    delay_hbm,
    out_ref,
    x,
    gram,
    stat_y,
    stat_z,
    power_y,
    power_z,
    table_v,
    table,
    thin,
    plane,
    left,
    right,
    final,
    coded,
    got,
    best,
    mask_ref,
    delay_ref,
    load_sem,
    small_sem,
    table_sem,
    halo_send,
    halo_recv,
    ring_send,
    ring_recv,
    swap_send,
    swap_recv,
    own_sem,
):
    tiles, own = geo.tiles, geo.own
    sub_index = lax.axis_index("sub")
    tm_index = lax.axis_index("tm")
    z_index, y_index = tm_index // geo.ny, lax.rem(tm_index, geo.ny)
    position = reversed_bits(sub_index, 3)
    n_tm = geo.ny * geo.nz
    not_first = tm_index > 0
    not_last = tm_index < n_tm - 1
    lane = iota((8, LANES), 1)
    place = iota((8, LANES), 0)

    def along_y(peer):
        return {"tm": z_index * geo.ny + peer}

    def along_z(peer):
        return {"tm": peer * geo.ny + y_index}

    barrier = pltpu.get_barrier_semaphore()
    for k in range(1, geo.ny):
        pl.semaphore_signal(barrier, inc=1, device_id=along_y(lax.rem(y_index + k, geo.ny)), device_id_type=MESH)
    for k in range(1, geo.nz):
        pl.semaphore_signal(barrier, inc=1, device_id=along_z(lax.rem(z_index + k, geo.nz)), device_id_type=MESH)
    for k in range(1, geo.n_sub):
        pl.semaphore_signal(
            barrier, inc=1, device_id={"sub": lax.rem(sub_index + k, geo.n_sub)}, device_id_type=MESH
        )
    for k in (1, n_tm - 1):
        pl.semaphore_signal(barrier, inc=1, device_id={"tm": lax.rem(tm_index + k, n_tm)}, device_id_type=MESH)

    own_first = LEFT * LANES
    right_first = (LEFT + own) * LANES
    chunk = geo.samples // 4
    loads = []
    for i in range(4):
        loads.append(
            pltpu.make_async_copy(
                spectra_ref.at[:, pl.ds(i * chunk, chunk)],
                x.at[:, pl.ds(own_first + i * chunk, chunk)],
                load_sem.at[i],
            )
        )
        loads[-1].start()
    small = [
        pltpu.make_async_copy(mask_hbm, mask_ref, small_sem.at[0]),
        pltpu.make_async_copy(delay_hbm, delay_ref, small_sem.at[1]),
    ]
    for copy in small:
        copy.start()

    sums = jnp.zeros((8, geo.channels), F32)
    nt = (((1,), (1,)), ((), ()))
    for i in range(4):
        loads[i].wait()
        part = x[:, pl.ds(own_first + i * chunk, chunk)]
        square = lax.dot_general(part, part, nt, preferred_element_type=F32)
        if i == 0:
            gram[...] = square
        else:
            gram[...] += square
        sums = sums + lax.dot_general(jnp.ones((8, chunk), BF16), part, nt, preferred_element_type=F32)
    diagonal = iota((geo.channels, geo.channels), 0) == iota((geo.channels, geo.channels), 1)
    squares = jnp.sum(jnp.where(diagonal, gram[...], 0.0), axis=0, keepdims=True)
    half = geo.channels // 2
    stats = jnp.concatenate(
        [sums[0:1, :half], sums[0:1, half:], squares[:, :half], squares[:, half:]], axis=0
    )
    pl.semaphore_wait(barrier, geo.ny + geo.nz + geo.n_sub - 1)
    over_y = Ring(stat_y, y_index, geo.ny, along_y, ring_send.at[0], ring_recv.at[0])
    over_z = Ring(stat_z, z_index, geo.nz, along_z, ring_send.at[1], ring_recv.at[1])
    over_y.start(stats)

    def to_prev():
        return remote(
            spectra_ref.at[:, pl.ds(0, RIGHT * LANES)],
            x.at[:, pl.ds(right_first, RIGHT * LANES)],
            halo_send.at[0],
            halo_recv.at[0],
            {"tm": tm_index - 1},
        )

    def to_next():
        return remote(
            spectra_ref.at[:, pl.ds(geo.samples - LEFT * LANES, LEFT * LANES)],
            x.at[:, pl.ds(0, LEFT * LANES)],
            halo_send.at[1],
            halo_recv.at[1],
            {"tm": tm_index + 1},
        )

    @pl.when(not_first)
    def _():
        to_prev().start()

    @pl.when(not_last)
    def _():
        to_next().start()

    @pl.when(jnp.logical_not(not_first))
    def _():
        x[:, pl.ds(0, LEFT * LANES)] = jnp.zeros((geo.channels, LEFT * LANES), BF16)

    @pl.when(jnp.logical_not(not_last))
    def _():
        x[:, pl.ds(right_first, RIGHT * LANES)] = jnp.zeros((geo.channels, RIGHT * LANES), BF16)

    thin[pl.ds(32 * tiles, 64), :] = jnp.zeros((64, LANES), F32)

    for copy in small:
        copy.wait()
    table_v[...] = delay_table(geo, position, sub_index, delay_ref)
    table_copy = pltpu.make_async_copy(table_v, table, table_sem)
    table_copy.start()
    over_z.start(over_y.total())

    totals = over_z.total()
    table_copy.wait()
    total_time = geo.samples * n_tm
    centre = jnp.concatenate([totals[0:1], totals[1:2]], axis=1) / total_time
    power = jnp.concatenate([totals[2:3], totals[3:4]], axis=1) / total_time
    spread = lax.rsqrt(power - centre * centre + 1e-05)
    weight = spread * mask_ref[...].astype(F32)
    bands = geo.channels // 8
    member = iota((bands, geo.channels), 1) // 8 == iota((bands, geo.channels), 0)
    gain = jnp.where(member, weight, 0.0)
    gain_1 = gain.astype(BF16)
    rest = gain - gain_1.astype(F32)
    gain_2 = rest.astype(BF16)
    gain_3 = (rest - gain_2.astype(F32)).astype(BF16)
    gains = jnp.concatenate([gain_1, gain_2, gain_3], axis=0)
    offset = -jnp.sum(gain * centre, axis=1, keepdims=True)

    def normalise(first, count, shift):
        sample = jnp.dot(gains, x[:, pl.ds(first * LANES, count * LANES)], preferred_element_type=F32)
        value = sample[:bands] + sample[bands : 2 * bands] + sample[2 * bands :] + shift
        for g in range(bands // 8):
            for j in range(count):
                thin[pl.ds(8 * g * tiles + first + j, 8, stride=tiles), :] = value[
                    8 * g : 8 * g + 8, j * LANES : (j + 1) * LANES
                ]

    for i in range(own // 4):
        normalise(LEFT + 4 * i, 4, offset)

    @pl.when(not_first)
    def _():
        to_prev().wait_send()
        to_next().wait_recv()

    @pl.when(not_last)
    def _():
        to_next().wait_send()
        to_prev().wait_recv()

    normalise(0, LEFT, jnp.where(not_first, offset, 0.0))
    normalise(LEFT + own, RIGHT, jnp.where(not_last, offset, 0.0))

    first_merge(geo, thin, plane, table)
    pairs = SPAN // 2

    def swap(k, peer, slot):
        return remote(coded.at[peer], got.at[slot], swap_send.at[k], swap_recv.at[slot], {"sub": peer})

    keep = pltpu.make_async_copy(coded.at[sub_index], got.at[position], own_sem)

    def piece(block, j):
        return pl.ds(pl.multiple_of(8 * (block * SPAN + j), 8), 8)

    def column(j):
        return slice(j * LANES, (j + 1) * LANES)

    def encode(peer):
        powers = jnp.zeros((8, LANES), F32)
        for j in range(pairs):
            one = right[piece(peer, j), :]
            two = right[piece(peer, j + pairs), :]
            largest = jnp.max(jnp.maximum(jnp.abs(one), jnp.abs(two)), axis=1, keepdims=True)
            power = jnp.ceil(jnp.log2(jnp.maximum(largest, 1e-30) * 1.001))
            factor = jnp.exp2(15.0 - power)
            code = jnp.concatenate([one * factor, two * factor], axis=0)
            coded[pl.ds(peer, 1), :, column(j)] = jnp.round(code).astype(I32).astype(jnp.int16)[None]
            powers = jnp.where(lane == j, power, powers)
        powers = jnp.concatenate([powers, powers], axis=0)
        coded[pl.ds(peer, 1), :, column(pairs)] = powers.astype(I32).astype(jnp.int16)[None]

    near = sub_index // 4
    far = 1 - near
    place_in_half = lax.rem(sub_index, 4)
    for half, first in ((far, 0), (near, 4)):
        merge(geo, plane, left, table, 5, 4, half)
        merge(geo, left, right, table, 6, 8, half)
        merge(geo, right, left, table, 7, 16, half)
        merge(geo, left, right, table, 8, 32, half)

        def send(k, carry):
            peer = 4 * half + lax.rem(place_in_half + k, 4)
            encode(peer)
            if first == 0:
                swap(first + k, peer, position).start()
            else:

                @pl.when(k < 4)
                def _():
                    swap(first + k, peer, position).start()

                @pl.when(k == 4)
                def _():
                    keep.start()

            return carry

        if first == 0:
            lax.fori_loop(0, 4, send, 0)
        else:
            lax.fori_loop(1, 5, send, 0)

    def decode(slot):
        block = got[pl.ds(slot, 1), :, column(pairs)]
        scales = jnp.exp2(jnp.reshape(block, (16, LANES)).astype(F32)[0:8] - 15.0)
        for j in range(pairs):
            code = jnp.reshape(got[pl.ds(slot, 1), :, column(j)], (16, LANES)).astype(F32)
            scale = along(scales, jnp.full((8, LANES), j, I32), 1)
            plane[piece(slot, j), :] = code[0:8] * scale
            plane[piece(slot, j + pairs), :] = code[8:16] * scale

    keep.wait()
    decode(position)

    def receive(source):
        slot = reversed_bits(source, 3)
        swap(0, source, slot).wait_recv()
        decode(slot)

    def receive_far(k, carry):
        receive(4 * far + lax.rem(place_in_half + 4 - k, 4))
        return carry

    def receive_near(k, carry):
        receive(4 * near + lax.rem(place_in_half + 4 - k, 4))
        return carry

    lax.fori_loop(0, 4, receive_far, 0)
    lax.fori_loop(1, 4, receive_near, 0)

    merge(geo, plane, left, table, 9, 8)
    merge(geo, left, right, table, 10, 16)
    merge(geo, right, final, table, 11, 32, to_step=tiles)

    def group_tile(g, j):
        return final[pl.ds(8 * g * tiles + j, 8, stride=tiles), :]

    def group_power(g, packed):
        total = jnp.zeros((8, LANES), F32)
        for j in range(LEFT, LEFT + own):
            tile = group_tile(g, j)
            total = total + tile * tile
        return jnp.where(lane == 8 * g + place, jnp.sum(total, axis=1, keepdims=True), packed)

    packed = lax.fori_loop(0, 8, group_power, jnp.zeros((8, LANES), F32), unroll=8)
    rings = [over_y, over_z]
    over_y = Ring(power_y, y_index, geo.ny, along_y, ring_send.at[2], ring_recv.at[2])
    over_z = Ring(power_z, z_index, geo.nz, along_z, ring_send.at[3], ring_recv.at[3])
    over_y.start(jnp.sum(packed, axis=0, keepdims=True))

    def group_best(g, carry):
        box = [jnp.where(not_first, group_tile(g, 0), 0.0)]
        box += [group_tile(g, j) for j in range(1, LEFT + own)]
        kept = jnp.zeros((8, LANES), F32)
        for section in range(WIDTHS):
            if section > 0:
                lag = 2 ** (section - 1)
                near = lane < LANES - lag
                for j in range(LEFT + own - 1, -1, -1):
                    mixed = jnp.where(near, box[j], box[max(j - 1, 0)])
                    box[j] = box[j] + pltpu.roll(mixed, lag, 1)
            found = [jnp.maximum(box[LEFT + 2 * b], box[LEFT + 2 * b + 1]) for b in range(own // 2)]
            step = 1
            while len(found) > 1:
                even = (lane & step) == 0
                found = [
                    jnp.maximum(jnp.where(even, a, b), pltpu.roll(jnp.where(even, b, a), step, 1))
                    for a, b in zip(found[::2], found[1::2])
                ]
                step *= 2
            largest = found[0]
            while step < LANES:
                largest = jnp.maximum(largest, pltpu.roll(largest, step, 1))
                step *= 2
            kept = jnp.where((lane >> 4) == section, largest * (1.0 / math.sqrt(2**section)), kept)
        best[pl.ds(pl.multiple_of(8 * g, 8), 8), :] = kept
        return carry

    lax.fori_loop(0, 4, group_best, 0, unroll=2)
    over_z.start(over_y.total())
    lax.fori_loop(4, 8, group_best, 0, unroll=2)
    for k in (0, 1, 2, 3, 5, 6, 7):
        swap(k, 4 * (far if k < 4 else near) + lax.rem(place_in_half + k, 4), position).wait_send()
    mean_power = over_z.total() / total_time
    for ring in rings + [over_y, over_z]:
        ring.sent()
    inverse = jnp.broadcast_to(1.0 / jnp.sqrt(mean_power + 1e-06), (8, LANES))
    for g in range(8):
        scale = jnp.sum(jnp.where(lane == 8 * g + place, inverse, 0.0), axis=1, keepdims=True)
        best[8 * g : 8 * g + 8, :] = best[8 * g : 8 * g + 8, :] * scale
    out_ref[...] = best[...].T


class Geometry:
    pass


def local(mesh, spectra, chan_mask, delay_step):
    geo = Geometry()
    geo.n_sub = mesh.shape["sub"]
    n_tm = mesh.shape["tm"]
    geo.ny = 4
    geo.nz = n_tm // geo.ny
    geo.channels, geo.samples = spectra.shape
    geo.own = geo.samples // LANES
    geo.tiles = LEFT + geo.own + RIGHT
    assert (geo.n_sub, geo.channels, geo.own, geo.ny * geo.nz) == (8, 256, 32, n_tm)
    dma = pltpu.SemaphoreType.DMA
    slots = max(geo.ny, geo.nz)
    width = geo.tiles * LANES
    geo.rows, geo.local_levels, geo.cross_levels = 64, 8, 3
    anywhere = pl.BlockSpec(memory_space=pl.ANY)
    best = pl.pallas_call(
        functools.partial(kernel, geo),
        out_shape=jax.ShapeDtypeStruct((WIDTHS * geo.own // 2, 64), F32),
        in_specs=[anywhere, anywhere, anywhere],
        out_specs=pl.BlockSpec(memory_space=pltpu.VMEM),
        scratch_shapes=[
            pltpu.VMEM((geo.channels, width), BF16),
            pltpu.VMEM((geo.channels, geo.channels), F32),
            pltpu.VMEM((geo.ny, 4, LANES), F32),
            pltpu.VMEM((geo.nz, 4, LANES), F32),
            pltpu.VMEM((geo.ny, 1, LANES), F32),
            pltpu.VMEM((geo.nz, 1, LANES), F32),
            pltpu.VMEM((8, LANES), I32),
            pltpu.SMEM((8, LANES), I32),
            pltpu.VMEM((32 * geo.tiles + 64, LANES), F32),
            pltpu.VMEM((64 * SPAN + 16, LANES), F32),
            pltpu.VMEM((64 * SPAN + 16, LANES), F32),
            pltpu.VMEM((64 * SPAN + 16, LANES), F32),
            pltpu.VMEM((64 * geo.tiles + 64, LANES), F32),
            pltpu.VMEM((8, 16, (SPAN // 2 + 1) * LANES), jnp.int16),
            pltpu.VMEM((8, 16, (SPAN // 2 + 1) * LANES), jnp.int16),
            pltpu.VMEM((64, LANES), F32),
            pltpu.VMEM((1, geo.channels), I32),
            pltpu.VMEM((16, LANES), I32),
            dma((4,)),
            dma((2,)),
            dma(()),
            dma((2,)),
            dma((2,)),
            dma((4, slots)),
            dma((4, slots)),
            dma((geo.n_sub,)),
            dma((geo.n_sub,)),
            dma(()),
        ],
        compiler_params=pltpu.CompilerParams(collective_id=0, has_side_effects=True, vmem_limit_bytes=62 * 2**20),
        name="dedisperse",
    )(spectra, chan_mask.reshape(1, geo.channels), delay_step.reshape(16, LANES))
    return best.reshape(WIDTHS, geo.own // 2, 64).transpose(2, 0, 1)


def solution(mesh):
    in_specs = (P("sub", "tm"), P("sub"), P())
    out_specs = P("sub", None, "tm")
    return jax.shard_map(
        functools.partial(local, mesh), mesh=mesh, in_specs=in_specs, out_specs=out_specs, check_vma=False
    )
```
